32 devices in a mesh: front: 4 (over z), row: 4 (over x, core), col: 2 (over y).
Axes of the slice: x: 2, y: 2, z: 4, core: 2. Of those that a mesh axis runs over, the one named last changes fastest.
Arguments:
- own_rows: float32 [4, 1536, 4096], P('front', 'row', 'col'), may hold values from -1.5 to 1.5
- child_rows: float32 [8192, 4096], P(('front', 'row'), 'col'), may hold values from -3 to 3
- child_dest: int32 [8192, 1], P(('front', 'row')), may hold values from 0 to 3; in each aligned block of 512 rows (0 to 511, 512 to 1023, ...) at most 256 rows name the same one
- child_stair: int32 [8192], P(('front', 'row')), may hold values from 0 to 7
Outputs:
- r_factor: float32 [4, 1024, 4096], P('front', 'row', 'col')
The draws below stay inside these ranges and needn't reach their ends.
Inputs may be any that keep to these rules, and one draw needn't show every extreme that they name: `child_dest`: among the 512 rows of one device at most 256 name one parent, and in every draw some device has exactly 256 rows for some parent.
All inputs are finite; a program needn't handle non-finite values.
Results may differ from the reference program's by a relative error of at most 0.0003.
Values sent between devices are 32-bit elements; how exact they have to be, the bound alone decides.
A program may use at most 128 MiB of HBM per device.

```python
import math
import jax
import jax.numpy as jnp
import numpy as np
from jax import lax

NC = 4096
PANEL_COLUMNS = 512
PANEL_COUNT = 2
SRC_DEV = 512
STAIR_BLK = 128
CAP = 256
OWN_ALL = 1536
CHILD_ROWS = 8192
N_FRONT = 4
N_ROW = 4


def place_ends(drawn, stream_key, least, high):
    longest = drawn.shape.index(max(drawn.shape))
    spots = []
    for shift in (0, 1):
        where = [jax.random.randint(jax.random.fold_in(stream_key, axis), (), 0, length) for axis, length in enumerate(drawn.shape)]
        where[longest] = (where[longest] + shift) % drawn.shape[longest]
        spots.append(tuple(where))
    return drawn.at[spots[0]].set(least).at[spots[1]].set(high)


def block_scale(key, dims, split, low, top_value):
    def one(dim, blocks):
        heights = jax.random.uniform(jax.random.fold_in(jax.random.fold_in(key, 6), dim), (blocks,), jnp.float32, low / len(split), top_value / len(split))
        return jnp.repeat(jnp.exp(heights), dims[dim] // blocks).reshape((-1,) + (1,) * (len(dims) - dim - 1))

    level = one(*split[0])
    for cut in split[1:]:
        level = level * one(*cut)
    return level


def deal_out(stream_key, own, number, rows, count, top, limit, lean):
    ranking = jax.random.permutation(stream_key, count)
    packed, ordinary = portions_of(count, rows * top, limit, lean, True), portions_of(count, rows * top, limit, lean, False)
    places = jnp.arange(count)

    def named(tallies, offset_by):
        used = int((tallies > 0).sum())
        fixed = max(1, used // 4)
        passed = fixed + (places - fixed + offset_by * (used - fixed)) % max(1, count - fixed)
        return jnp.zeros((count,), jnp.int32).at[ranking[jnp.where(places < fixed, places, passed)]].set(jnp.asarray(tallies, jnp.int32))

    tallies = jnp.where(number % 4 == 0, named(packed, number // 4), named(ordinary, number - number // 4 - 1))
    mixed = jax.random.permutation(jax.random.fold_in(own, 3), count)
    giver, receiver = mixed[0:count // 2 * 2:2], mixed[1:count // 2 * 2:2]
    margin = jnp.minimum(tallies[giver] - 1, limit - tallies[receiver]) // 2
    margin = jnp.where((giver == ranking[0]) | (receiver == ranking[0]) | (tallies[receiver] == 0), 0, jnp.maximum(margin, 0))
    passed = jax.random.randint(jax.random.fold_in(own, 4), (count // 2,), 0, 1 << 20) % (margin + 1)
    tallies = tallies.at[giver].add(-passed).at[receiver].add(passed)
    labels = jnp.searchsorted(jnp.cumsum(tallies), jnp.arange(rows * top), side="right").astype(jnp.int32)
    grid = labels.reshape(top, rows).T
    grid = grid[jax.random.permutation(jax.random.fold_in(own, 1), rows)]
    offset_by = jax.random.randint(jax.random.fold_in(own, 2), (rows, 1), 0, top)
    return jnp.take_along_axis(grid, (jnp.arange(top)[None, :] + offset_by) % top, axis=1)


def portions_of(number_of, total, reach, slope, full):
    weights = [(1 << 20) // math.isqrt(grade ** slope) + 1 for grade in range(1, number_of + 1)]
    largest = reach if full else min(reach, max(-(-total // number_of), total * weights[0] // sum(weights)))
    least = 1 if total - largest >= number_of - 1 else 0
    counts, rest = [largest] + [least] * (number_of - 1), total - largest - least * (number_of - 1)
    while rest > 0:
        free = [i for i in range(1, number_of) if counts[i] < largest] or [i for i in range(1, number_of) if counts[i] < reach]
        whole, remaining = sum([weights[i] for i in free]), rest
        for i in free:
            extra = min(reach - counts[i], max(1, remaining * weights[i] // whole), rest)
            counts[i] = counts[i] + extra
            rest = rest - extra
    return np.array(counts)


def bell_draw(own_key, extent, width, most, pieces=(), kind=jnp.bfloat16):
    result = jax.random.normal(own_key, extent, jnp.float32) * width
    if len(pieces) > 0:
        result = block_scale(own_key, extent, pieces, -0.22, 0.18) * result
    return jnp.clip(result, min=-most, max=most).astype(kind)


def setup_inputs(seed: int = 0) -> dict:
    keys = jax.random.split(jax.random.key(seed), 5)
    own_rows = bell_draw(keys[0], (N_FRONT, OWN_ALL, NC), 0.25, 1.5, ((0, 4), (1, 4), (2, 2)), jnp.float32)
    child_rows = bell_draw(keys[1], (CHILD_ROWS, NC), 0.5, 3.0, ((0, 16), (1, 2)), jnp.float32)
    child_dest_keys = jax.random.split(jax.random.fold_in(keys[2], 1), CHILD_ROWS // SRC_DEV)
    child_dest_turns = jax.random.permutation(jax.random.fold_in(keys[2], 3), CHILD_ROWS // SRC_DEV)
    child_dest = jax.vmap(lambda own, number: deal_out(jax.random.fold_in(keys[2], 2), own, number, SRC_DEV, N_FRONT, 1, CAP, 1))(child_dest_keys, child_dest_turns).reshape((CHILD_ROWS, 1))
    child_stair = place_ends(jax.random.randint(keys[3], (CHILD_ROWS,), 0, 8), jax.random.fold_in(keys[3], 1), 0, 7).astype(jnp.int32)
    return {"own_rows": own_rows, "child_rows": child_rows, "child_dest": child_dest, "child_stair": child_stair}


def reference(own_rows, child_rows, child_dest, child_stair):
    columns = jnp.arange(NC, dtype=jnp.int32)
    kept_mask = columns[None, :] >= (child_stair * STAIR_BLK)[:, None]
    masked_rows = jnp.where(kept_mask, child_rows, jnp.zeros_like(child_rows))
    targets = child_dest[:, 0]
    bound_rows = N_FRONT * N_ROW * CAP
    eliminated_panel = PANEL_COUNT * PANEL_COLUMNS

    def one_parent(parent):
        hits = targets == parent
        position = jnp.nonzero(hits, size=bound_rows, fill_value=0)[0].astype(jnp.int32)
        is_valid = jnp.arange(bound_rows, dtype=jnp.int32) < jnp.sum(hits.astype(jnp.int32))
        picked_rows = jnp.where(is_valid[:, None], masked_rows[position], jnp.zeros((bound_rows, NC), masked_rows.dtype))
        stacked_rows = jnp.concatenate([own_rows[parent], picked_rows], 0)
        gramian_block = jnp.dot(stacked_rows[:, :eliminated_panel].T, stacked_rows, precision=lax.Precision.HIGHEST, preferred_element_type=masked_rows.dtype)
        lower_cholesky_factor = jnp.linalg.cholesky(gramian_block[:, :eliminated_panel])
        return jax.scipy.linalg.solve_triangular(lower_cholesky_factor, gramian_block, lower=True)
    return lax.map(one_parent, jnp.arange(N_FRONT, dtype=jnp.int32))
```

```python
import functools
import jax
import jax.numpy as jnp
from jax import lax
from jax.experimental import pallas as pl
from jax.experimental.pallas import tpu as pltpu
from jax.sharding import PartitionSpec as P

PANEL_COLUMNS = 512
PANEL_COUNT = 2
STAIR_BLK = 128
BLOCK = 128
HALF = 64
TILE = 256
PIECE = 64
HI = lax.Precision.HIGHEST
TN = (((0,), (0,)), ((), ()))
NN = (((1,), (0,)), ((), ()))
MESH = pl.DeviceIdType.MESH


def mm(a, b, dims=NN):
    return lax.dot_general(a, b, dims, precision=HI, preferred_element_type=jnp.float32)


def split(x):
    hi = x.astype(jnp.bfloat16)
    return hi, (x - hi.astype(jnp.float32)).astype(jnp.bfloat16)


def dot3(a, b, dims):
    a_hi, a_lo = a
    b_hi, b_lo = b

    def dot(x, y):
        return lax.dot_general(x, y, dims, preferred_element_type=jnp.float32)

    return dot(a_lo, b_hi) + dot(a_hi, b_lo) + dot(a_hi, b_hi)


def shift_order(n):
    return sorted(range(1, n), key=lambda s: (-min(s, n - s), s))


def square_tiles(eliminated, n_col):
    tiles = eliminated // TILE
    packed = [(i, k) for i in range(tiles) for k in range(i, tiles)]
    return [packed[c::n_col] for c in range(n_col)]


def pick(col, values):
    out = values[0]
    for c in range(1, len(values)):
        out = jnp.where(col == c, values[c], out)
    return out


def remote(src, dst, send_sem, recv_sem, device):
    return pltpu.make_async_remote_copy(
        src_ref=src,
        dst_ref=dst,
        send_sem=send_sem,
        recv_sem=recv_sem,
        device_id=device,
        device_id_type=MESH,
    )


def front_kernel(
    n_front, n_col, cap, own, send, prod, square,
    rows, pan, hi, lo, zs, zr, ys, yr, here_sem,
):
    f = lax.axis_index("front")
    c = lax.axis_index("col")
    n_own, width = own.shape
    eliminated = pan.shape[1]
    order = [0] + shift_order(n_front)
    piece = min(PIECE, cap)
    per = cap // piece
    first = n_own + cap
    count = (n_front - 1) * per

    barrier = pltpu.get_barrier_semaphore()
    for s in range(1, n_front):
        pl.semaphore_signal(
            barrier, inc=1, device_id={"front": (f + s) % n_front}, device_id_type=MESH
        )
    for s in range(1, n_col):
        pl.semaphore_signal(
            barrier, inc=1, device_id={"col": (c + s) % n_col}, device_id_type=MESH
        )

    local = [
        pltpu.make_async_copy(own, rows.at[pl.ds(0, n_own)], here_sem.at[0]),
        pltpu.make_async_copy(
            send.at[pl.ds(0, cap)], rows.at[pl.ds(n_own, cap)], here_sem.at[1]
        ),
    ]
    for copy in local:
        copy.start()
    pl.semaphore_wait(barrier, n_front - 1 + n_col - 1)

    def z_copy(j, target):
        return remote(
            send.at[pl.ds(pl.multiple_of(cap + j * piece, piece), piece)],
            rows.at[pl.ds(pl.multiple_of(first + j * piece, piece), piece)],
            zs.at[j],
            zr.at[j],
            {"front": target},
        )

    for j in range(count):
        z_copy(j, (f + order[1 + j // per]) % n_front).start()

    def y_copy(slot, start, size, other):
        return remote(
            rows.at[pl.ds(start, size), pl.ds(0, eliminated)],
            pan.at[pl.ds(start, size)],
            ys.at[slot, other],
            yr.at[slot],
            {"col": other},
        )

    prod[...] = jnp.zeros_like(prod)
    square[...] = jnp.zeros_like(square)
    lists = square_tiles(eliminated, n_col)

    def consume(slot, start, size):
        @pl.when(c == 0)
        def _():
            for other in range(1, n_col):
                y_copy(slot, start, size, other).start()
            h, l = split(rows[pl.ds(start, size), pl.ds(0, eliminated)])
            hi[pl.ds(0, size)] = h
            lo[pl.ds(0, size)] = l

        @pl.when(c > 0)
        def _():
            y_copy(slot, start, size, 1).wait_recv()
            h, l = split(pan[pl.ds(start, size)])
            hi[pl.ds(0, size)] = h
            lo[pl.ds(0, size)] = l

        def lhs(i):
            at = pl.ds(pl.multiple_of(i * TILE, TILE), TILE)
            return hi[pl.ds(0, size), at], lo[pl.ds(0, size), at]

        def column(n, carry):
            at = pl.ds(pl.multiple_of(n * TILE, TILE), TILE)
            rhs = split(rows[pl.ds(start, size), at])
            for i in range(eliminated // TILE):
                prod[pl.ds(i * TILE, TILE), at] += dot3(lhs(i), rhs, TN)
            return carry

        lax.fori_loop(0, width // TILE, column, 0)
        for j in range(len(lists[0])):
            a = pick(c, [t[min(j, len(t) - 1)][0] for t in lists])
            b = pick(c, [t[min(j, len(t) - 1)][1] for t in lists])
            square[j] += dot3(lhs(a), lhs(b), TN)

    local[0].wait()
    consume(0, 0, n_own)
    local[1].wait()
    consume(1, n_own, cap)

    def arrived(j, carry):
        z_copy(j, f).wait_recv()
        consume(2 + j, pl.multiple_of(first + j * piece, piece), piece)
        return carry

    lax.fori_loop(0, count, arrived, 0)

    @pl.when(c == 0)
    def _():
        for other in range(1, n_col):
            y_copy(0, 0, n_own, other).wait_send()
            y_copy(1, n_own, cap, other).wait_send()

            def sent(j, carry):
                start = pl.multiple_of(first + j * piece, piece)
                y_copy(2 + j, start, piece, other).wait_send()
                return carry

            lax.fori_loop(0, count, sent, 0)

    def left(j, carry):
        z_copy(j, f).wait_send()
        return carry

    lax.fori_loop(0, count, left, 0)


def front_gram(own, send, n_front, n_col, cap, eliminated):
    n_own, width = own.shape
    total = n_own + n_front * cap
    piece = min(PIECE, cap)
    count = (n_front - 1) * (cap // piece)
    slots = len(square_tiles(eliminated, n_col)[0])
    most = max(n_own, cap)
    return pl.pallas_call(
        functools.partial(front_kernel, n_front, n_col, cap),
        out_shape=(
            jax.ShapeDtypeStruct((eliminated, width), jnp.float32),
            jax.ShapeDtypeStruct((slots, TILE, TILE), jnp.float32),
        ),
        in_specs=[pl.BlockSpec(memory_space=pl.ANY)] * 2,
        out_specs=(pl.BlockSpec(memory_space=pltpu.VMEM),) * 2,
        scratch_shapes=[
            pltpu.VMEM((total, width), jnp.float32),
            pltpu.VMEM((total, eliminated), jnp.float32),
            pltpu.VMEM((most, eliminated), jnp.bfloat16),
            pltpu.VMEM((most, eliminated), jnp.bfloat16),
            pltpu.SemaphoreType.DMA((count,)),
            pltpu.SemaphoreType.DMA((count,)),
            pltpu.SemaphoreType.DMA((count + 2, n_col)),
            pltpu.SemaphoreType.DMA((count + 2,)),
            pltpu.SemaphoreType.DMA((2,)),
        ],
        compiler_params=pltpu.CompilerParams(
            collective_id=0, has_side_effects=True, vmem_limit_bytes=60 << 20
        ),
    )(own, send)


def small_inverse(block):
    lanes = lax.broadcasted_iota(jnp.int32, (HALF, HALF), 1)
    rows = lax.broadcasted_iota(jnp.int32, (HALF, HALF), 0)
    eye = (lanes == rows).astype(jnp.float32)
    both = jnp.concatenate([block, eye], 1)
    count = HALF // 8
    groups = [both[g * 8 : (g + 1) * 8] for g in range(count)]
    sub = lax.broadcasted_iota(jnp.int32, (8, 2 * HALF), 0)

    def column_of(g, j):
        return jnp.broadcast_to(groups[g][:, j : j + 1], (8, 2 * HALF))

    def row_of(x, s):
        return jnp.broadcast_to(x[s : s + 1], x.shape)

    for home in range(count):
        first = home * 8
        below = [[column_of(g, first + s) for s in range(8)] for g in range(home + 1, count)]
        columns = [column_of(home, first + s) for s in range(8)]
        solved = forward = groups[home]
        pivots = columns[0]
        for s in range(8):
            column = columns[s]
            pivot = row_of(column, s)
            inverse = 1.0 / pivot
            pivots = jnp.where(sub == s, pivot, pivots)
            forward = jnp.where(
                sub > s, forward - column * (row_of(forward, s) * inverse), forward
            )
            scaled = row_of(solved, s) * inverse
            solved = jnp.where(sub == s, scaled, solved - column * scaled)
            for t in range(s + 1, 8):
                scaled = row_of(columns[t], s) * inverse
                columns[t] = jnp.where(sub == s, scaled, columns[t] - column * scaled)
        groups[home] = forward * lax.rsqrt(pivots)
        spread = [row_of(solved, s) for s in range(8)]
        for g in range(home + 1, count):
            terms = [below[g - home - 1][s] * spread[s] for s in range(8)]
            while len(terms) > 1:
                terms = [terms[i] + terms[i + 1] for i in range(0, len(terms), 2)]
            groups[g] = groups[g] - terms[0]
    return jnp.concatenate(groups, 0)[:, HALF:]


def block_inverse(d):
    first = small_inverse(d[:HALF, :HALF])
    r12 = mm(first, d[:HALF, HALF:])
    second = small_inverse(d[HALF:, HALF:] - mm(r12, r12, TN))
    corner = -mm(second, mm(r12, first, TN))
    return jnp.concatenate(
        [
            jnp.concatenate([first, jnp.zeros((HALF, HALF), jnp.float32)], 1),
            jnp.concatenate([corner, second], 1),
        ],
        0,
    )


def tail_kernel(
    n_row, n_col, prod, square, out,
    part, other, whole_sq, work, near, leave, far, mine, ready,
    s1, s2, s3, s4, s5, r1, r2, ro_s, ro_r,
):
    r = lax.axis_index("row")
    c = lax.axis_index("col")
    eliminated, width = prod.shape
    share = width // n_row
    slots = square.shape[0]
    low = r % 2
    high = r // 2
    mate = r + 1 - 2 * low
    across = r + 2 - 4 * high
    y = n_col - 1 - c
    count = eliminated // BLOCK
    owner_rows = eliminated // n_row
    half = TILE // 2

    barrier = pltpu.get_barrier_semaphore()
    for s in range(1, n_row):
        pl.semaphore_signal(
            barrier, inc=1, device_id={"row": (r + s) % n_row}, device_id_type=MESH
        )
    pl.semaphore_signal(barrier, inc=1, device_id={"col": y}, device_id_type=MESH)
    pl.semaphore_wait(barrier, n_row)

    kept = pl.ds(pl.multiple_of(low * half, half), half)
    given = pl.ds(pl.multiple_of((1 - low) * half, half), half)

    def core_copy(j):
        return remote(square.at[j, given], part.at[j], s1.at[0, j], s1.at[1, j], {"row": mate})

    def x_copy(j):
        return remote(part.at[slots + j], other.at[j], s2.at[0, j], s2.at[1, j], {"row": across})

    def y_copy(j, col):
        tile = whole_sq.at[n_col * j + col, kept]
        return remote(tile, tile, s3.at[0, j], s3.at[1, j], {"col": y})

    def y_recv(j):
        tile = whole_sq.at[n_col * j + y, kept]
        return remote(tile, tile, s3.at[0, j], s3.at[1, j], {"col": y})

    def mate_copy(j, col, sems):
        tile = whole_sq.at[n_col * j + col, kept]
        return remote(tile, tile, sems.at[0, j], sems.at[1, j], {"row": mate})

    def mate_recv(j, col, sems):
        tile = whole_sq.at[n_col * j + col, given]
        return remote(tile, tile, sems.at[0, j], sems.at[1, j], {"row": mate})

    def near_copy(q):
        at = pl.ds(pl.multiple_of((2 * q + 1 - low) * share, share), share)
        return remote(prod.at[:, at], near.at[q], r1.at[0, q], r1.at[1, q], {"row": mate})

    def far_copy(k):
        at = pl.ds(pl.multiple_of(k * BLOCK, BLOCK), BLOCK)
        return remote(leave.at[at], far.at[at], r2.at[0, k], r2.at[1, k], {"row": across})

    for j in range(slots):
        core_copy(j).start()
    for q in range(n_row // 2):
        near_copy(q).start()
    for j in range(slots):
        core_copy(j).wait_recv()
        part[slots + j] = square[j, kept] + part[j]
        x_copy(j).start()
    for j in range(slots):
        x_copy(j).wait_recv()
        whole_sq[n_col * j + c, kept] = part[slots + j] + other[j]
        y_copy(j, c).start()
        mate_copy(j, c, s4).start()
    for q in range(n_row // 2):
        near_copy(q).wait_recv()

    def gather(k, carry):
        at = pl.ds(pl.multiple_of(k * BLOCK, BLOCK), BLOCK)
        theirs = pl.ds(pl.multiple_of((2 * (1 - high) + low) * share, share), share)
        ours = pl.ds(pl.multiple_of((2 * high + low) * share, share), share)
        leave[at] = prod[at, theirs] + near[1 - high, at]
        far_copy(k).start()
        mine[at] = prod[at, ours] + near[high, at]
        return carry

    lax.fori_loop(0, count, gather, 0)
    for j in range(slots):
        y_recv(j).wait_recv()
        mate_copy(j, y, s5).start()
    for j in range(slots):
        mate_recv(j, c, s4).wait_recv()
        mate_recv(j, y, s5).wait_recv()

    lists = square_tiles(eliminated, n_col)
    for col in range(n_col):
        for j, (a, b) in enumerate(lists[col]):
            work[a * TILE : (a + 1) * TILE, b * TILE : (b + 1) * TILE] = whole_sq[n_col * j + col]

    lanes = lax.broadcasted_iota(jnp.int32, (BLOCK, eliminated), 1)

    def result_copy(k):
        at = pl.ds(pl.multiple_of(k * BLOCK, BLOCK), BLOCK)
        owner = k * BLOCK // owner_rows
        inside = pl.ds(pl.multiple_of(k * BLOCK % owner_rows, BLOCK), BLOCK)
        cols = pl.ds(pl.multiple_of(r * share, share), share)
        return remote(
            ready.at[at],
            out.at[inside, cols],
            ro_s.at[k],
            ro_r.at[r, k % (owner_rows // BLOCK)],
            {"row": owner},
        )

    def result_recv(source, k):
        inside = pl.ds(k * BLOCK, BLOCK)
        cols = pl.ds(pl.multiple_of(source * share, share), share)
        return remote(
            ready.at[inside],
            out.at[inside, cols],
            ro_s.at[k],
            ro_r.at[source, k],
            {"row": source},
        )

    def outer(k, carry):
        r0 = pl.multiple_of(k * BLOCK, BLOCK)
        at = pl.ds(r0, BLOCK)
        whole = block_inverse(work[at, at])
        here = (lanes >= r0) & (lanes < r0 + BLOCK)
        top = dot3(split(whole), split(work[at, :]), NN)
        work[at, :] = top
        work[at, at] = whole

        def inner(j, carry):
            s0 = pl.multiple_of(j * BLOCK, BLOCK)
            to = pl.ds(s0, BLOCK)
            left = split(work[at, to])
            right = split(work[at, :])
            keep = jnp.where(here, 0.0, work[to, :])
            work[to, :] = keep - dot3(left, right, TN)
            return carry

        lax.fori_loop(k + 1, count, inner, 0)

        far_copy(k).wait_recv()
        mine[at] += far[at]

        def term(m, acc):
            to = pl.ds(pl.multiple_of(m * BLOCK, BLOCK), BLOCK)
            return acc + dot3(split(work[at, to]), split(mine[to]), NN)

        ready[at] = lax.fori_loop(0, k + 1, term, jnp.zeros((BLOCK, share), jnp.float32))
        owner = k * BLOCK // owner_rows

        @pl.when(owner == r)
        def _():
            inside = pl.ds(pl.multiple_of(k * BLOCK % owner_rows, BLOCK), BLOCK)
            out[inside, pl.ds(pl.multiple_of(r * share, share), share)] = ready[at]

        @pl.when(owner != r)
        def _():
            result_copy(k).start()

        return carry

    lax.fori_loop(0, count, outer, 0)

    for s in range(1, n_row):
        for k in range(owner_rows // BLOCK):
            result_recv((r + s) % n_row, k).wait_recv()

    def sent(k, carry):
        far_copy(k).wait_send()

        @pl.when(k * BLOCK // owner_rows != r)
        def _():
            result_copy(k).wait_send()

        return carry

    lax.fori_loop(0, count, sent, 0)
    for j in range(slots):
        core_copy(j).wait_send()
        x_copy(j).wait_send()
        y_copy(j, c).wait_send()
        mate_copy(j, c, s4).wait_send()
        mate_copy(j, y, s5).wait_send()
    for q in range(n_row // 2):
        near_copy(q).wait_send()


def tail(prod, square, n_row, n_col):
    eliminated, width = prod.shape
    share = width // n_row
    slots = square.shape[0]
    count = eliminated // BLOCK
    owner_rows = eliminated // n_row
    half = TILE // 2
    dma = pltpu.SemaphoreType.DMA
    return pl.pallas_call(
        functools.partial(tail_kernel, n_row, n_col),
        out_shape=jax.ShapeDtypeStruct((owner_rows, width), jnp.float32),
        in_specs=[pl.BlockSpec(memory_space=pltpu.VMEM)] * 2,
        out_specs=pl.BlockSpec(memory_space=pltpu.VMEM),
        scratch_shapes=[
            pltpu.VMEM((2 * slots, half, TILE), jnp.float32),
            pltpu.VMEM((slots, half, TILE), jnp.float32),
            pltpu.VMEM((n_col * slots, TILE, TILE), jnp.float32),
            pltpu.VMEM((eliminated, eliminated), jnp.float32),
            pltpu.VMEM((n_row // 2, eliminated, share), jnp.float32),
            pltpu.VMEM((eliminated, share), jnp.float32),
            pltpu.VMEM((eliminated, share), jnp.float32),
            pltpu.VMEM((eliminated, share), jnp.float32),
            pltpu.VMEM((eliminated, share), jnp.float32),
            dma((2, slots)),
            dma((2, slots)),
            dma((2, slots)),
            dma((2, slots)),
            dma((2, slots)),
            dma((2, n_row // 2)),
            dma((2, count)),
            dma((count,)),
            dma((n_row, owner_rows // BLOCK)),
        ],
        compiler_params=pltpu.CompilerParams(
            collective_id=1, has_side_effects=True, vmem_limit_bytes=60 << 20
        ),
    )(prod, square)


def body(own_rows, child_rows, child_dest, child_stair):
    n_front = lax.axis_size("front")
    n_row = lax.axis_size("row")
    n_col = lax.axis_size("col")
    source_rows, half_cols = child_rows.shape
    capacity = max(2, 2 * source_rows // n_front)
    col_index = lax.axis_index("col")
    global_cols = col_index * half_cols + lax.broadcasted_iota(
        jnp.int32, (source_rows, half_cols), 1
    )
    masked_rows = jnp.where(global_cols >= (child_stair * STAIR_BLK)[:, None], child_rows, 0.0)
    targets = child_dest[:, 0]
    onehot = (targets[:, None] == jnp.arange(n_front, dtype=jnp.int32)[None, :]).astype(jnp.int32)
    slot = jnp.sum((jnp.cumsum(onehot, axis=0) - onehot) * onehot, axis=1)
    shift = (targets - lax.axis_index("front")) % n_front
    rank = jnp.zeros_like(shift)
    for place, s in enumerate(shift_order(n_front)):
        rank = jnp.where(shift == s, place + 1, rank)
    position = rank * capacity + slot
    send = jnp.zeros((n_front * capacity, half_cols), jnp.float32).at[position].set(masked_rows)
    eliminated = PANEL_COUNT * PANEL_COLUMNS
    prod, square = front_gram(own_rows[0], send, n_front, n_col, capacity, eliminated)
    return tail(prod, square, n_row, n_col)[None]


def solution(mesh):
    placed = (
        P("front", "row", "col"),
        P(("front", "row"), "col"),
        P(("front", "row"), None),
        P(("front", "row")),
    )
    return jax.shard_map(
        body, mesh=mesh, in_specs=placed, out_specs=P("front", "row", "col"), check_vma=False
    )
```

```python
import functools
import jax
import jax.numpy as jnp
from jax import lax
from jax.experimental import pallas as pl
from jax.experimental.pallas import tpu as pltpu
from jax.sharding import PartitionSpec as P

PANEL_COLUMNS = 512
PANEL_COUNT = 2
STAIR_BLK = 128
BLOCK = 128
HALF = 64
TILE = 256
PIECE = 64
CHUNK = 512
TN = (((0,), (0,)), ((), ()))
NN = (((1,), (0,)), ((), ()))
MESH = pl.DeviceIdType.MESH


def split(x):
    hi = x.astype(jnp.bfloat16)
    return hi, (x - hi.astype(jnp.float32)).astype(jnp.bfloat16)


def dot3(a, b, dims):
    a_hi, a_lo = a
    b_hi, b_lo = b

    def dot(x, y):
        return lax.dot_general(x, y, dims, preferred_element_type=jnp.float32)

    return dot(a_lo, b_hi) + dot(a_hi, b_lo) + dot(a_hi, b_hi)


def shift_order(n):
    return sorted(range(1, n), key=lambda s: (-min(s, n - s), s))


def square_tiles(eliminated, n_col):
    tiles = eliminated // TILE
    packed = [(i, k) for i in range(tiles) for k in range(i, tiles)]
    return [packed[c::n_col] for c in range(n_col)]


def pick(col, values):
    out = values[0]
    for c in range(1, len(values)):
        out = jnp.where(col == c, values[c], out)
    return out


def remote(src, dst, send_sem, recv_sem, device):
    return pltpu.make_async_remote_copy(
        src_ref=src,
        dst_ref=dst,
        send_sem=send_sem,
        recv_sem=recv_sem,
        device_id=device,
        device_id_type=MESH,
    )


def front_kernel(
    n_front, n_col, cap, own, send, prod, square,
    rows, pan, hi, lo, zs, zr, ys, yr, here_sem,
):
    f = lax.axis_index("front")
    c = lax.axis_index("col")
    n_own, width = own.shape
    eliminated = pan.shape[1]
    order = [0] + shift_order(n_front)
    piece = min(PIECE, cap)
    per = cap // piece
    first = n_own + cap
    count = (n_front - 1) * per

    barrier = pltpu.get_barrier_semaphore()
    for s in range(1, n_front):
        pl.semaphore_signal(
            barrier, inc=1, device_id={"front": (f + s) % n_front}, device_id_type=MESH
        )
    for s in range(1, n_col):
        pl.semaphore_signal(
            barrier, inc=1, device_id={"col": (c + s) % n_col}, device_id_type=MESH
        )

    local = [
        pltpu.make_async_copy(own, rows.at[pl.ds(0, n_own)], here_sem.at[0]),
        pltpu.make_async_copy(
            send.at[pl.ds(0, cap)], rows.at[pl.ds(n_own, cap)], here_sem.at[1]
        ),
    ]
    for copy in local:
        copy.start()
    pl.semaphore_wait(barrier, n_front - 1 + n_col - 1)

    def z_copy(j, target):
        return remote(
            send.at[pl.ds(pl.multiple_of(cap + j * piece, piece), piece)],
            rows.at[pl.ds(pl.multiple_of(first + j * piece, piece), piece)],
            zs.at[j],
            zr.at[j],
            {"front": target},
        )

    for j in range(count):
        z_copy(j, (f + order[1 + j // per]) % n_front).start()

    groups = list(range(n_front - 1))
    late = sorted(groups, key=lambda q: (-min(order[1 + q], n_front - order[1 + q]), -q))

    def y_copy(slot, start, size, other):
        return remote(
            rows.at[pl.ds(start, size), pl.ds(0, eliminated)],
            pan.at[pl.ds(start, size)],
            ys.at[slot, other],
            yr.at[slot],
            {"col": other},
        )

    prod[...] = jnp.zeros_like(prod)
    square[...] = jnp.zeros_like(square)
    lists = square_tiles(eliminated, n_col)

    def consume(slot, start, size):
        @pl.when(c == 0)
        def _():
            for other in range(1, n_col):
                y_copy(slot, start, size, other).start()
            h, l = split(rows[pl.ds(start, size), pl.ds(0, eliminated)])
            hi[pl.ds(0, size)] = h
            lo[pl.ds(0, size)] = l

        @pl.when(c > 0)
        def _():
            y_copy(slot, start, size, 1).wait_recv()
            h, l = split(pan[pl.ds(start, size)])
            hi[pl.ds(0, size)] = h
            lo[pl.ds(0, size)] = l

        def lhs(i):
            at = pl.ds(pl.multiple_of(i * TILE, TILE), TILE)
            return hi[pl.ds(0, size), at], lo[pl.ds(0, size), at]

        def column(n, carry):
            at = pl.ds(pl.multiple_of(n * TILE, TILE), TILE)
            rhs = split(rows[pl.ds(start, size), at])
            for i in range(eliminated // TILE):
                prod[pl.ds(i * TILE, TILE), at] += dot3(lhs(i), rhs, TN)
            return carry

        lax.fori_loop(0, width // TILE, column, 0)
        for j in range(len(lists[0])):
            a = pick(c, [t[min(j, len(t) - 1)][0] for t in lists])
            b = pick(c, [t[min(j, len(t) - 1)][1] for t in lists])
            square[j] += dot3(lhs(a), lhs(b), TN)

    local[0].wait()
    consume(0, 0, n_own)
    local[1].wait()
    consume(1, n_own, cap)

    def arrived(i, carry):
        group = jnp.where(2 * f < n_front, i // per, pick(i // per, late))
        j = group * per + i % per
        z_copy(j, f).wait_recv()
        consume(2 + j, pl.multiple_of(first + j * piece, piece), piece)
        return carry

    lax.fori_loop(0, count, arrived, 0)

    @pl.when(c == 0)
    def _():
        for other in range(1, n_col):
            y_copy(0, 0, n_own, other).wait_send()
            y_copy(1, n_own, cap, other).wait_send()

            def sent(j, carry):
                start = pl.multiple_of(first + j * piece, piece)
                y_copy(2 + j, start, piece, other).wait_send()
                return carry

            lax.fori_loop(0, count, sent, 0)

    def left(j, carry):
        z_copy(j, f).wait_send()
        return carry

    lax.fori_loop(0, count, left, 0)


def front_gram(own, send, n_front, n_col, cap, eliminated):
    n_own, width = own.shape
    total = n_own + n_front * cap
    piece = min(PIECE, cap)
    count = (n_front - 1) * (cap // piece)
    slots = len(square_tiles(eliminated, n_col)[0])
    most = max(n_own, cap)
    return pl.pallas_call(
        functools.partial(front_kernel, n_front, n_col, cap),
        out_shape=(
            jax.ShapeDtypeStruct((eliminated, width), jnp.float32),
            jax.ShapeDtypeStruct((slots, TILE, TILE), jnp.float32),
        ),
        in_specs=[pl.BlockSpec(memory_space=pl.ANY)] * 2,
        out_specs=(pl.BlockSpec(memory_space=pltpu.VMEM),) * 2,
        scratch_shapes=[
            pltpu.VMEM((total, width), jnp.float32),
            pltpu.VMEM((total, eliminated), jnp.float32),
            pltpu.VMEM((most, eliminated), jnp.bfloat16),
            pltpu.VMEM((most, eliminated), jnp.bfloat16),
            pltpu.SemaphoreType.DMA((count,)),
            pltpu.SemaphoreType.DMA((count,)),
            pltpu.SemaphoreType.DMA((count + 2, n_col)),
            pltpu.SemaphoreType.DMA((count + 2,)),
            pltpu.SemaphoreType.DMA((2,)),
        ],
        compiler_params=pltpu.CompilerParams(
            collective_id=0, has_side_effects=True, vmem_limit_bytes=60 << 20
        ),
    )(own, send)


def small_inverse(block):
    lanes = lax.broadcasted_iota(jnp.int32, (HALF, HALF), 1)
    rows = lax.broadcasted_iota(jnp.int32, (HALF, HALF), 0)
    eye = (lanes == rows).astype(jnp.float32)
    both = jnp.concatenate([block, eye], 1)
    count = HALF // 8
    groups = [both[g * 8 : (g + 1) * 8] for g in range(count)]
    sub = lax.broadcasted_iota(jnp.int32, (8, 2 * HALF), 0)

    def column_of(g, j):
        return jnp.broadcast_to(groups[g][:, j : j + 1], (8, 2 * HALF))

    def row_of(x, s):
        return jnp.broadcast_to(x[s : s + 1], x.shape)

    for home in range(count):
        first = home * 8
        below = [[column_of(g, first + s) for s in range(8)] for g in range(home + 1, count)]
        columns = [column_of(home, first + s) for s in range(8)]
        solved = forward = groups[home]
        pivot = row_of(columns[0], 0)
        pivots = pivot
        for s in range(8):
            column = columns[s]
            inverse = 1.0 / pivot
            pivots = jnp.where(sub == s, pivot, pivots)
            forward = jnp.where(
                sub > s, forward - column * (row_of(forward, s) * inverse), forward
            )
            scaled = row_of(solved, s) * inverse
            solved = jnp.where(sub == s, scaled, solved - column * scaled)
            for t in range(s + 1, 8):
                row = row_of(columns[t], s)
                fresh = columns[t] - (column * row) * inverse
                if t == s + 1:
                    pivot = row_of(fresh, t)
                columns[t] = jnp.where(sub == s, row * inverse, fresh)
        groups[home] = forward * lax.rsqrt(pivots)
        spread = [row_of(solved, s) for s in range(8)]
        for g in range(home + 1, count):
            terms = [below[g - home - 1][s] * spread[s] for s in range(8)]
            while len(terms) > 1:
                terms = [terms[i] + terms[i + 1] for i in range(0, len(terms), 2)]
            groups[g] = groups[g] - terms[0]
    return jnp.concatenate(groups, 0)[:, HALF:]


def block_inverse(d):
    first = small_inverse(d[:HALF, :HALF])
    first_parts = split(first)
    r12 = dot3(first_parts, split(d[:HALF, HALF:]), NN)
    r12_parts = split(r12)
    second = small_inverse(d[HALF:, HALF:] - dot3(r12_parts, r12_parts, TN))
    corner = -dot3(split(second), split(dot3(r12_parts, first_parts, TN)), NN)
    return jnp.concatenate(
        [
            jnp.concatenate([first, jnp.zeros((HALF, HALF), jnp.float32)], 1),
            jnp.concatenate([corner, second], 1),
        ],
        0,
    )


def tail_kernel(
    n_row, n_col, prod, square, out,
    part, other, whole_sq, work, near, leave, far, ready,
    prev_hi, prev_lo,
    s1, s2, s3, s4, s5, r1, r2, ro_s, ro_r,
):
    r = lax.axis_index("row")
    c = lax.axis_index("col")
    eliminated, width = prod.shape
    share = width // n_row
    slots = square.shape[0]
    low = r % 2
    high = r // 2
    mate = r + 1 - 2 * low
    across = r + 2 - 4 * high
    y = n_col - 1 - c
    count = eliminated // BLOCK
    owner_rows = eliminated // n_row
    half = TILE // 2

    barrier = pltpu.get_barrier_semaphore()
    for s in range(1, n_row):
        pl.semaphore_signal(
            barrier, inc=1, device_id={"row": (r + s) % n_row}, device_id_type=MESH
        )
    pl.semaphore_signal(barrier, inc=1, device_id={"col": y}, device_id_type=MESH)
    pl.semaphore_wait(barrier, n_row)

    kept = pl.ds(pl.multiple_of(low * half, half), half)
    given = pl.ds(pl.multiple_of((1 - low) * half, half), half)

    def core_copy(j):
        return remote(square.at[j, given], part.at[j], s1.at[0, j], s1.at[1, j], {"row": mate})

    def x_copy(j):
        return remote(part.at[slots + j], other.at[j], s2.at[0, j], s2.at[1, j], {"row": across})

    def y_copy(j, col):
        tile = whole_sq.at[n_col * j + col, kept]
        return remote(tile, tile, s3.at[0, j], s3.at[1, j], {"col": y})

    def y_recv(j):
        tile = whole_sq.at[n_col * j + y, kept]
        return remote(tile, tile, s3.at[0, j], s3.at[1, j], {"col": y})

    def mate_copy(j, col, sems):
        tile = whole_sq.at[n_col * j + col, kept]
        return remote(tile, tile, sems.at[0, j], sems.at[1, j], {"row": mate})

    def mate_recv(j, col, sems):
        tile = whole_sq.at[n_col * j + col, given]
        return remote(tile, tile, sems.at[0, j], sems.at[1, j], {"row": mate})

    def near_copy(q):
        at = pl.ds(pl.multiple_of((2 * q + 1 - low) * share, share), share)
        return remote(prod.at[:, at], near.at[q], r1.at[0, q], r1.at[1, q], {"row": mate})

    def far_copy(k):
        at = pl.ds(pl.multiple_of(k * BLOCK, BLOCK), BLOCK)
        return remote(leave.at[at], far.at[at], r2.at[0, k], r2.at[1, k], {"row": across})

    for j in range(slots):
        core_copy(j).start()
    for q in range(n_row // 2):
        near_copy(q).start()
    for j in range(slots):
        core_copy(j).wait_recv()
        part[slots + j] = square[j, kept] + part[j]
        x_copy(j).start()
    for j in range(slots):
        x_copy(j).wait_recv()
        whole_sq[n_col * j + c, kept] = part[slots + j] + other[j]
        y_copy(j, c).start()
        mate_copy(j, c, s4).start()
    for q in range(n_row // 2):
        near_copy(q).wait_recv()

    def gather(k, carry):
        at = pl.ds(pl.multiple_of(k * BLOCK, BLOCK), BLOCK)
        theirs = pl.ds(pl.multiple_of((2 * (1 - high) + low) * share, share), share)
        ours = pl.ds(pl.multiple_of((2 * high + low) * share, share), share)
        leave[at] = prod[at, theirs] + near[1 - high, at]
        far_copy(k).start()
        work[at, pl.ds(eliminated, share)] = prod[at, ours] + near[high, at]
        return carry

    lax.fori_loop(0, count, gather, 0)
    for j in range(slots):
        y_recv(j).wait_recv()
        mate_copy(j, y, s5).start()
    for j in range(slots):
        mate_recv(j, c, s4).wait_recv()
        mate_recv(j, y, s5).wait_recv()

    lists = square_tiles(eliminated, n_col)
    for col in range(n_col):
        for j, (a, b) in enumerate(lists[col]):
            work[a * TILE : (a + 1) * TILE, b * TILE : (b + 1) * TILE] = whole_sq[n_col * j + col]

    def result_copy(k):
        at = pl.ds(pl.multiple_of(k * BLOCK, BLOCK), BLOCK)
        owner = k * BLOCK // owner_rows
        inside = pl.ds(pl.multiple_of(k * BLOCK % owner_rows, BLOCK), BLOCK)
        cols = pl.ds(pl.multiple_of(r * share, share), share)
        return remote(
            ready.at[at],
            out.at[inside, cols],
            ro_s.at[k],
            ro_r.at[r, k % (owner_rows // BLOCK)],
            {"row": owner},
        )

    def result_recv(source, k):
        inside = pl.ds(k * BLOCK, BLOCK)
        cols = pl.ds(pl.multiple_of(source * share, share), share)
        return remote(
            ready.at[inside],
            out.at[inside, cols],
            ro_s.at[k],
            ro_r.at[source, k],
            {"row": source},
        )

    def deliver(k):
        at = pl.ds(pl.multiple_of(k * BLOCK, BLOCK), BLOCK)
        owner = k * BLOCK // owner_rows

        @pl.when(owner == r)
        def _():
            inside = pl.ds(pl.multiple_of(k * BLOCK % owner_rows, BLOCK), BLOCK)
            out[inside, pl.ds(pl.multiple_of(r * share, share), share)] = ready[at]

        @pl.when(owner != r)
        def _():
            result_copy(k).start()

    lanes = lax.broadcasted_iota(jnp.int32, (BLOCK, eliminated), 1)
    total = eliminated + share

    def outer(k, carry):
        at = pl.ds(pl.multiple_of(k * BLOCK, BLOCK), BLOCK)
        scale = split(block_inverse(work[at, at]))
        far_copy(k).wait_recv()
        result = dot3(scale, split(work[at, eliminated:] + far[at]), NN)
        ready[at] = result
        prev_hi[:, eliminated:], prev_lo[:, eliminated:] = split(result)
        top = dot3(scale, split(work[at, :eliminated]), NN)
        top = jnp.where(lanes >= (k + 1) * BLOCK, top, 0.0)
        prev_hi[:, :eliminated], prev_lo[:, :eliminated] = split(top)
        deliver(k)

        def inner(j, carry):
            rows = pl.ds(pl.multiple_of(j * BLOCK, BLOCK), BLOCK)
            left = prev_hi[:, rows], prev_lo[:, rows]
            for start in range(0, total, CHUNK):
                cols = slice(start, min(total, start + CHUNK))

                @pl.when(j * BLOCK < cols.stop)
                def _():
                    work[rows, cols] -= dot3(left, (prev_hi[:, cols], prev_lo[:, cols]), TN)

            return carry

        lax.fori_loop(k + 1, count, inner, 0)
        return carry

    lax.fori_loop(0, count, outer, 0)

    for s in range(1, n_row):
        for k in range(owner_rows // BLOCK):
            result_recv((r + s) % n_row, k).wait_recv()

    def sent(k, carry):
        far_copy(k).wait_send()

        @pl.when(k * BLOCK // owner_rows != r)
        def _():
            result_copy(k).wait_send()

        return carry

    lax.fori_loop(0, count, sent, 0)
    for j in range(slots):
        core_copy(j).wait_send()
        x_copy(j).wait_send()
        y_copy(j, c).wait_send()
        mate_copy(j, c, s4).wait_send()
        mate_copy(j, y, s5).wait_send()
    for q in range(n_row // 2):
        near_copy(q).wait_send()


def tail(prod, square, n_row, n_col):
    eliminated, width = prod.shape
    share = width // n_row
    slots = square.shape[0]
    count = eliminated // BLOCK
    owner_rows = eliminated // n_row
    half = TILE // 2
    dma = pltpu.SemaphoreType.DMA
    return pl.pallas_call(
        functools.partial(tail_kernel, n_row, n_col),
        out_shape=jax.ShapeDtypeStruct((owner_rows, width), jnp.float32),
        in_specs=[pl.BlockSpec(memory_space=pltpu.VMEM)] * 2,
        out_specs=pl.BlockSpec(memory_space=pltpu.VMEM),
        scratch_shapes=[
            pltpu.VMEM((2 * slots, half, TILE), jnp.float32),
            pltpu.VMEM((slots, half, TILE), jnp.float32),
            pltpu.VMEM((n_col * slots, TILE, TILE), jnp.float32),
            pltpu.VMEM((eliminated, eliminated + share), jnp.float32),
            pltpu.VMEM((n_row // 2, eliminated, share), jnp.float32),
            pltpu.VMEM((eliminated, share), jnp.float32),
            pltpu.VMEM((eliminated, share), jnp.float32),
            pltpu.VMEM((eliminated, share), jnp.float32),
            pltpu.VMEM((BLOCK, eliminated + share), jnp.bfloat16),
            pltpu.VMEM((BLOCK, eliminated + share), jnp.bfloat16),
            dma((2, slots)),
            dma((2, slots)),
            dma((2, slots)),
            dma((2, slots)),
            dma((2, slots)),
            dma((2, n_row // 2)),
            dma((2, count)),
            dma((count,)),
            dma((n_row, owner_rows // BLOCK)),
        ],
        compiler_params=pltpu.CompilerParams(
            collective_id=1, has_side_effects=True, vmem_limit_bytes=60 << 20
        ),
    )(prod, square)


def body(own_rows, child_rows, child_dest, child_stair):
    n_front = lax.axis_size("front")
    n_row = lax.axis_size("row")
    n_col = lax.axis_size("col")
    source_rows, half_cols = child_rows.shape
    capacity = max(2, 2 * source_rows // n_front)
    col_index = lax.axis_index("col")
    global_cols = col_index * half_cols + lax.broadcasted_iota(
        jnp.int32, (source_rows, half_cols), 1
    )
    masked_rows = jnp.where(global_cols >= (child_stair * STAIR_BLK)[:, None], child_rows, 0.0)
    targets = child_dest[:, 0]
    onehot = (targets[:, None] == jnp.arange(n_front, dtype=jnp.int32)[None, :]).astype(jnp.int32)
    slot = jnp.sum((jnp.cumsum(onehot, axis=0) - onehot) * onehot, axis=1)
    shift = (targets - lax.axis_index("front")) % n_front
    rank = jnp.zeros_like(shift)
    for place, s in enumerate(shift_order(n_front)):
        rank = jnp.where(shift == s, place + 1, rank)
    position = rank * capacity + slot
    send = jnp.zeros((n_front * capacity, half_cols), jnp.float32).at[position].set(masked_rows)
    eliminated = PANEL_COUNT * PANEL_COLUMNS
    prod, square = front_gram(own_rows[0], send, n_front, n_col, capacity, eliminated)
    return tail(prod, square, n_row, n_col)[None]


def solution(mesh):
    placed = (
        P("front", "row", "col"),
        P(("front", "row"), "col"),
        P(("front", "row"), None),
        P(("front", "row")),
    )
    return jax.shard_map(
        body, mesh=mesh, in_specs=placed, out_specs=P("front", "row", "col"), check_vma=False
    )
```

```python
import functools
import jax
import jax.numpy as jnp
from jax import lax
from jax.experimental import pallas as pl
from jax.experimental.pallas import tpu as pltpu
from jax.sharding import PartitionSpec as P

PANEL_COLUMNS = 512
PANEL_COUNT = 2
STAIR_BLK = 128
STAIRS = 8
BLOCK = 128
HALF = 64
TILE = 256
PIECE = 64
CHUNK = 512
TN = (((0,), (0,)), ((), ()))
NN = (((1,), (0,)), ((), ()))
MESH = pl.DeviceIdType.MESH


def split(x):
    hi = x.astype(jnp.bfloat16)
    return hi, (x - hi.astype(jnp.float32)).astype(jnp.bfloat16)


def dot(a, b, dims):
    return lax.dot_general(a, b, dims, preferred_element_type=jnp.float32)


def dot3(a, b, dims):
    a_hi, a_lo = a
    b_hi, b_lo = b
    return dot(a_lo, b_hi, dims) + dot(a_hi, b_lo, dims) + dot(a_hi, b_hi, dims)


def left_of(x, axis=0):
    hi, lo = split(x)
    return jnp.concatenate([lo, hi, hi], axis)


def right_of(x):
    hi, lo = split(x)
    return jnp.concatenate([hi, lo, hi], 0)


def shift_order(n):
    return sorted(range(1, n), key=lambda s: (-min(s, n - s), s))


def square_tiles(eliminated, n_col):
    tiles = eliminated // TILE
    packed = [(i, k) for i in range(tiles) for k in range(i, tiles)]
    return [packed[c::n_col] for c in range(n_col)]


def pick(col, values):
    out = values[0]
    for c in range(1, len(values)):
        out = jnp.where(col == c, values[c], out)
    return out


def remote(src, dst, send_sem, recv_sem, device):
    return pltpu.make_async_remote_copy(
        src_ref=src,
        dst_ref=dst,
        send_sem=send_sem,
        recv_sem=recv_sem,
        device_id=device,
        device_id_type=MESH,
    )


def front_kernel(
    n_front, n_col, cap, codes, own, child, prod, square,
    rows, pan, lhs, source, parcel, zs, zr, ys, yr, here_sem,
):
    f = lax.axis_index("front")
    c = lax.axis_index("col")
    n_own, width = own.shape
    eliminated = pan.shape[1]
    order = [0] + shift_order(n_front)
    piece = min(PIECE, cap)
    per = cap // piece
    first = n_own + cap
    count = (n_front - 1) * per

    local = [
        pltpu.make_async_copy(child, source, here_sem.at[0]),
        pltpu.make_async_copy(own, rows.at[pl.ds(0, n_own)], here_sem.at[1]),
    ]
    for copy in local:
        copy.start()
    barrier = pltpu.get_barrier_semaphore()
    for s in range(1, n_front):
        pl.semaphore_signal(
            barrier, inc=1, device_id={"front": (f + s) % n_front}, device_id_type=MESH
        )
    for s in range(1, n_col):
        pl.semaphore_signal(
            barrier, inc=1, device_id={"col": (c + s) % n_col}, device_id_type=MESH
        )
    pl.semaphore_wait(barrier, n_front - 1 + n_col - 1)

    def z_copy(j, target):
        return remote(
            parcel.at[pl.ds(pl.multiple_of(j * piece, piece), piece)],
            rows.at[pl.ds(pl.multiple_of(first + j * piece, piece), piece)],
            zs.at[j],
            zr.at[j],
            {"front": target},
        )

    groups = list(range(n_front - 1))
    late = sorted(groups, key=lambda q: (-min(order[1 + q], n_front - order[1 + q]), -q))

    def y_copy(slot, start, size, other):
        return remote(
            rows.at[pl.ds(start, size), pl.ds(0, eliminated)],
            pan.at[pl.ds(start, size)],
            ys.at[slot, other],
            yr.at[slot],
            {"col": other},
        )

    columns = c * width + lax.broadcasted_iota(jnp.int32, (1, width), 1)

    def pack(into, start, code_start, size):
        def one(i, carry):
            code = codes[code_start + i] - 1
            row = source[pl.ds(jnp.maximum(code, 0) // STAIRS, 1), :]
            edge = jnp.where(code < 0, n_col * width, code % STAIRS * STAIR_BLK)
            into[pl.ds(start + i, 1), :] = jnp.where(columns >= edge, row, 0.0)
            return carry

        lax.fori_loop(0, size, one, 0, unroll=4)

    local[0].wait()

    def post(j, carry):
        pack(parcel, j * piece, cap + j * piece, piece)
        z_copy(j, (f + pick(j // per, order[1:])) % n_front).start()
        return carry

    lax.fori_loop(0, count, post, 0)
    pack(rows, n_own, 0, cap)

    prod[...] = jnp.zeros_like(prod)
    square[...] = jnp.zeros_like(square)
    lists = square_tiles(eliminated, n_col)

    def consume(slot, start, size):
        @pl.when(c == 0)
        def _():
            for other in range(1, n_col):
                y_copy(slot, start, size, other).start()
            lhs[pl.ds(0, 3 * size)] = left_of(rows[pl.ds(start, size), pl.ds(0, eliminated)])

        @pl.when(c > 0)
        def _():
            y_copy(slot, start, size, 1).wait_recv()
            lhs[pl.ds(0, 3 * size)] = left_of(pan[pl.ds(start, size)])

        def column(n, carry):
            at = pl.ds(pl.multiple_of(n * TILE, TILE), TILE)
            rhs = right_of(rows[pl.ds(start, size), at])
            for i in range(eliminated // TILE):
                tile = pl.ds(i * TILE, TILE)
                prod[tile, at] += dot(lhs[pl.ds(0, 3 * size), tile], rhs, TN)
            return carry

        lax.fori_loop(0, width // TILE, column, 0)
        for j in range(len(lists[0])):
            a = pick(c, [t[min(j, len(t) - 1)][0] for t in lists])
            b = pick(c, [t[min(j, len(t) - 1)][1] for t in lists])
            row = pl.ds(pl.multiple_of(a * TILE, TILE), TILE)
            col = pl.ds(pl.multiple_of(b * TILE, TILE), TILE)
            lo, hi = lhs[pl.ds(0, size), col], lhs[pl.ds(size, size), col]
            rhs = jnp.concatenate([hi, lo, hi], 0)
            square[j] += dot(lhs[pl.ds(0, 3 * size), row], rhs, TN)

    local[1].wait()
    consume(0, 0, n_own)
    consume(1, n_own, cap)

    def arrived(i, carry):
        group = jnp.where(2 * f < n_front, i // per, pick(i // per, late))
        j = group * per + i % per
        z_copy(j, f).wait_recv()
        consume(2 + j, pl.multiple_of(first + j * piece, piece), piece)
        return carry

    lax.fori_loop(0, count, arrived, 0)

    @pl.when(c == 0)
    def _():
        for other in range(1, n_col):
            y_copy(0, 0, n_own, other).wait_send()
            y_copy(1, n_own, cap, other).wait_send()

            def sent(j, carry):
                start = pl.multiple_of(first + j * piece, piece)
                y_copy(2 + j, start, piece, other).wait_send()
                return carry

            lax.fori_loop(0, count, sent, 0)

    def left(j, carry):
        z_copy(j, f).wait_send()
        return carry

    lax.fori_loop(0, count, left, 0)


def front_gram(codes, own, child, n_front, n_col, cap, eliminated):
    n_own, width = own.shape
    total = n_own + n_front * cap
    piece = min(PIECE, cap)
    count = (n_front - 1) * (cap // piece)
    slots = len(square_tiles(eliminated, n_col)[0])
    most = max(n_own, cap)
    return pl.pallas_call(
        functools.partial(front_kernel, n_front, n_col, cap),
        out_shape=(
            jax.ShapeDtypeStruct((eliminated, width), jnp.float32),
            jax.ShapeDtypeStruct((slots, TILE, TILE), jnp.float32),
        ),
        in_specs=[pl.BlockSpec(memory_space=pltpu.SMEM)] + [pl.BlockSpec(memory_space=pl.ANY)] * 2,
        out_specs=(pl.BlockSpec(memory_space=pltpu.VMEM),) * 2,
        scratch_shapes=[
            pltpu.VMEM((total, width), jnp.float32),
            pltpu.VMEM((total, eliminated), jnp.float32),
            pltpu.VMEM((3 * most, eliminated), jnp.bfloat16),
            pltpu.VMEM(child.shape, jnp.float32),
            pltpu.VMEM((count * piece, width), jnp.float32),
            pltpu.SemaphoreType.DMA((count,)),
            pltpu.SemaphoreType.DMA((count,)),
            pltpu.SemaphoreType.DMA((count + 2, n_col)),
            pltpu.SemaphoreType.DMA((count + 2,)),
            pltpu.SemaphoreType.DMA((2,)),
        ],
        compiler_params=pltpu.CompilerParams(
            collective_id=0, has_side_effects=True, vmem_limit_bytes=60 << 20
        ),
    )(codes, own, child)


def small_inverse(block):
    lanes = lax.broadcasted_iota(jnp.int32, (HALF, HALF), 1)
    rows = lax.broadcasted_iota(jnp.int32, (HALF, HALF), 0)
    eye = (lanes == rows).astype(jnp.float32)
    both = jnp.concatenate([block, eye], 1)
    count = HALF // 8
    groups = [both[g * 8 : (g + 1) * 8] for g in range(count)]
    sub = lax.broadcasted_iota(jnp.int32, (8, 2 * HALF), 0)

    def column_of(g, j):
        return jnp.broadcast_to(groups[g][:, j : j + 1], (8, 2 * HALF))

    def row_of(x, s):
        return jnp.broadcast_to(x[s : s + 1], x.shape)

    for home in range(count):
        first = home * 8
        below = [[column_of(g, first + s) for s in range(8)] for g in range(home + 1, count)]
        columns = [column_of(home, first + s) for s in range(8)]
        solved = forward = groups[home]
        pivot = row_of(columns[0], 0)
        pivots = pivot
        for s in range(8):
            column = columns[s]
            inverse = 1.0 / pivot
            pivots = jnp.where(sub == s, pivot, pivots)
            forward = jnp.where(
                sub > s, forward - column * (row_of(forward, s) * inverse), forward
            )
            scaled = row_of(solved, s) * inverse
            solved = jnp.where(sub == s, scaled, solved - column * scaled)
            for t in range(s + 1, 8):
                row = row_of(columns[t], s)
                fresh = columns[t] - (column * row) * inverse
                if t == s + 1:
                    pivot = row_of(fresh, t)
                columns[t] = jnp.where(sub == s, row * inverse, fresh)
        groups[home] = forward * lax.rsqrt(pivots)
        spread = [row_of(solved, s) for s in range(8)]
        for g in range(home + 1, count):
            terms = [below[g - home - 1][s] * spread[s] for s in range(8)]
            while len(terms) > 1:
                terms = [terms[i] + terms[i + 1] for i in range(0, len(terms), 2)]
            groups[g] = groups[g] - terms[0]
    return jnp.concatenate(groups, 0)[:, HALF:]


def block_inverse(d):
    first = small_inverse(d[:HALF, :HALF])
    first_parts = split(first)
    r12 = dot3(first_parts, split(d[:HALF, HALF:]), NN)
    r12_parts = split(r12)
    second = small_inverse(d[HALF:, HALF:] - dot3(r12_parts, r12_parts, TN))
    corner = -dot3(split(second), split(dot3(r12_parts, first_parts, TN)), NN)
    return jnp.concatenate(
        [
            jnp.concatenate([first, jnp.zeros((HALF, HALF), jnp.float32)], 1),
            jnp.concatenate([corner, second], 1),
        ],
        0,
    )


def tail_kernel(
    n_row, n_col, prod, square, out,
    part, other, whole_sq, work, near, leave, far, ready,
    prev,
    s1, s2, s3, s4, s5, r1, r2, ro_s, ro_r,
):
    r = lax.axis_index("row")
    c = lax.axis_index("col")
    eliminated, width = prod.shape
    share = width // n_row
    slots = square.shape[0]
    low = r % 2
    high = r // 2
    mate = r + 1 - 2 * low
    across = r + 2 - 4 * high
    y = n_col - 1 - c
    count = eliminated // BLOCK
    owner_rows = eliminated // n_row
    half = TILE // 2

    barrier = pltpu.get_barrier_semaphore()
    for s in range(1, n_row):
        pl.semaphore_signal(
            barrier, inc=1, device_id={"row": (r + s) % n_row}, device_id_type=MESH
        )
    pl.semaphore_signal(barrier, inc=1, device_id={"col": y}, device_id_type=MESH)
    pl.semaphore_wait(barrier, n_row)

    kept = pl.ds(pl.multiple_of(low * half, half), half)
    given = pl.ds(pl.multiple_of((1 - low) * half, half), half)

    def core_copy(j):
        return remote(square.at[j, given], part.at[j], s1.at[0, j], s1.at[1, j], {"row": mate})

    def x_copy(j):
        return remote(part.at[slots + j], other.at[j], s2.at[0, j], s2.at[1, j], {"row": across})

    def y_copy(j, col):
        tile = whole_sq.at[n_col * j + col, kept]
        return remote(tile, tile, s3.at[0, j], s3.at[1, j], {"col": y})

    def y_recv(j):
        tile = whole_sq.at[n_col * j + y, kept]
        return remote(tile, tile, s3.at[0, j], s3.at[1, j], {"col": y})

    def mate_copy(j, col, sems):
        tile = whole_sq.at[n_col * j + col, kept]
        return remote(tile, tile, sems.at[0, j], sems.at[1, j], {"row": mate})

    def mate_recv(j, col, sems):
        tile = whole_sq.at[n_col * j + col, given]
        return remote(tile, tile, sems.at[0, j], sems.at[1, j], {"row": mate})

    def near_copy(q):
        at = pl.ds(pl.multiple_of((2 * q + 1 - low) * share, share), share)
        return remote(prod.at[:, at], near.at[q], r1.at[0, q], r1.at[1, q], {"row": mate})

    def far_copy(k):
        at = pl.ds(pl.multiple_of(k * BLOCK, BLOCK), BLOCK)
        return remote(leave.at[at], far.at[at], r2.at[0, k], r2.at[1, k], {"row": across})

    for j in range(slots):
        core_copy(j).start()
    for q in range(n_row // 2):
        near_copy(q).start()
    for j in range(slots):
        core_copy(j).wait_recv()
        part[slots + j] = square[j, kept] + part[j]
        x_copy(j).start()
    for j in range(slots):
        x_copy(j).wait_recv()
        whole_sq[n_col * j + c, kept] = part[slots + j] + other[j]
        y_copy(j, c).start()
        mate_copy(j, c, s4).start()
    for q in range(n_row // 2):
        near_copy(q).wait_recv()

    def gather(k, carry):
        at = pl.ds(pl.multiple_of(k * BLOCK, BLOCK), BLOCK)
        theirs = pl.ds(pl.multiple_of((2 * (1 - high) + low) * share, share), share)
        ours = pl.ds(pl.multiple_of((2 * high + low) * share, share), share)
        leave[at] = prod[at, theirs] + near[1 - high, at]
        far_copy(k).start()
        work[at, pl.ds(eliminated, share)] = prod[at, ours] + near[high, at]
        return carry

    lax.fori_loop(0, count, gather, 0)
    for j in range(slots):
        y_recv(j).wait_recv()
        mate_copy(j, y, s5).start()
    for j in range(slots):
        mate_recv(j, c, s4).wait_recv()
        mate_recv(j, y, s5).wait_recv()

    lists = square_tiles(eliminated, n_col)
    for col in range(n_col):
        for j, (a, b) in enumerate(lists[col]):
            work[a * TILE : (a + 1) * TILE, b * TILE : (b + 1) * TILE] = whole_sq[n_col * j + col]

    def result_copy(k):
        at = pl.ds(pl.multiple_of(k * BLOCK, BLOCK), BLOCK)
        owner = k * BLOCK // owner_rows
        inside = pl.ds(pl.multiple_of(k * BLOCK % owner_rows, BLOCK), BLOCK)
        cols = pl.ds(pl.multiple_of(r * share, share), share)
        return remote(
            ready.at[at],
            out.at[inside, cols],
            ro_s.at[k],
            ro_r.at[r, k % (owner_rows // BLOCK)],
            {"row": owner},
        )

    def result_recv(source, k):
        inside = pl.ds(k * BLOCK, BLOCK)
        cols = pl.ds(pl.multiple_of(source * share, share), share)
        return remote(
            ready.at[inside],
            out.at[inside, cols],
            ro_s.at[k],
            ro_r.at[source, k],
            {"row": source},
        )

    def deliver(k):
        at = pl.ds(pl.multiple_of(k * BLOCK, BLOCK), BLOCK)
        owner = k * BLOCK // owner_rows

        @pl.when(owner == r)
        def _():
            inside = pl.ds(pl.multiple_of(k * BLOCK % owner_rows, BLOCK), BLOCK)
            out[inside, pl.ds(pl.multiple_of(r * share, share), share)] = ready[at]

        @pl.when(owner != r)
        def _():
            result_copy(k).start()

    lanes = lax.broadcasted_iota(jnp.int32, (BLOCK, eliminated), 1)
    total = eliminated + share

    def outer(k, carry):
        at = pl.ds(pl.multiple_of(k * BLOCK, BLOCK), BLOCK)
        scale = left_of(block_inverse(work[at, at]), 1)
        far_copy(k).wait_recv()
        result = dot(scale, right_of(work[at, eliminated:] + far[at]), NN)
        ready[at] = result
        prev[:, eliminated:] = right_of(result)
        top = dot(scale, right_of(work[at, :eliminated]), NN)
        top = jnp.where(lanes >= (k + 1) * BLOCK, top, 0.0)
        prev[:, :eliminated] = right_of(top)
        deliver(k)

        def inner(j, carry):
            rows = pl.ds(pl.multiple_of(j * BLOCK, BLOCK), BLOCK)
            hi, lo = prev[:BLOCK, rows], prev[BLOCK : 2 * BLOCK, rows]
            left = jnp.concatenate([lo, hi, hi], 0)
            for start in range(0, total, CHUNK):
                cols = slice(start, min(total, start + CHUNK))

                @pl.when(j * BLOCK < cols.stop)
                def _():
                    work[rows, cols] -= dot(left, prev[:, cols], TN)

            return carry

        lax.fori_loop(k + 1, count, inner, 0)
        return carry

    lax.fori_loop(0, count, outer, 0)

    for s in range(1, n_row):
        for k in range(owner_rows // BLOCK):
            result_recv((r + s) % n_row, k).wait_recv()

    def sent(k, carry):
        far_copy(k).wait_send()

        @pl.when(k * BLOCK // owner_rows != r)
        def _():
            result_copy(k).wait_send()

        return carry

    lax.fori_loop(0, count, sent, 0)
    for j in range(slots):
        core_copy(j).wait_send()
        x_copy(j).wait_send()
        y_copy(j, c).wait_send()
        mate_copy(j, c, s4).wait_send()
        mate_copy(j, y, s5).wait_send()
    for q in range(n_row // 2):
        near_copy(q).wait_send()


def tail(prod, square, n_row, n_col):
    eliminated, width = prod.shape
    share = width // n_row
    slots = square.shape[0]
    count = eliminated // BLOCK
    owner_rows = eliminated // n_row
    half = TILE // 2
    dma = pltpu.SemaphoreType.DMA
    return pl.pallas_call(
        functools.partial(tail_kernel, n_row, n_col),
        out_shape=jax.ShapeDtypeStruct((owner_rows, width), jnp.float32),
        in_specs=[pl.BlockSpec(memory_space=pltpu.VMEM)] * 2,
        out_specs=pl.BlockSpec(memory_space=pltpu.VMEM),
        scratch_shapes=[
            pltpu.VMEM((2 * slots, half, TILE), jnp.float32),
            pltpu.VMEM((slots, half, TILE), jnp.float32),
            pltpu.VMEM((n_col * slots, TILE, TILE), jnp.float32),
            pltpu.VMEM((eliminated, eliminated + share), jnp.float32),
            pltpu.VMEM((n_row // 2, eliminated, share), jnp.float32),
            pltpu.VMEM((eliminated, share), jnp.float32),
            pltpu.VMEM((eliminated, share), jnp.float32),
            pltpu.VMEM((eliminated, share), jnp.float32),
            pltpu.VMEM((3 * BLOCK, eliminated + share), jnp.bfloat16),
            dma((2, slots)),
            dma((2, slots)),
            dma((2, slots)),
            dma((2, slots)),
            dma((2, slots)),
            dma((2, n_row // 2)),
            dma((2, count)),
            dma((count,)),
            dma((n_row, owner_rows // BLOCK)),
        ],
        compiler_params=pltpu.CompilerParams(
            collective_id=1, has_side_effects=True, vmem_limit_bytes=60 << 20
        ),
    )(prod, square)


def body(own_rows, child_rows, child_dest, child_stair):
    n_front = lax.axis_size("front")
    n_row = lax.axis_size("row")
    n_col = lax.axis_size("col")
    source_rows = child_rows.shape[0]
    capacity = max(2, 2 * source_rows // n_front)
    targets = child_dest[:, 0]
    index = lax.iota(jnp.int32, source_rows)
    ahead = (targets[None, :] == targets[:, None]) & (index[None, :] < index[:, None])
    slot = jnp.sum(ahead.astype(jnp.int32), axis=1)
    shift = (targets - lax.axis_index("front")) % n_front
    rank = jnp.zeros_like(shift)
    for place, s in enumerate(shift_order(n_front)):
        rank = jnp.where(shift == s, place + 1, rank)
    position = rank * capacity + slot
    code = index * STAIRS + child_stair + 1
    places = lax.iota(jnp.int32, n_front * capacity)
    codes = jnp.sum(jnp.where(position[None, :] == places[:, None], code[None, :], 0), axis=1)
    eliminated = PANEL_COUNT * PANEL_COLUMNS
    prod, square = front_gram(
        codes, own_rows[0], child_rows, n_front, n_col, capacity, eliminated
    )
    return tail(prod, square, n_row, n_col)[None]


def solution(mesh):
    placed = (
        P("front", "row", "col"),
        P(("front", "row"), "col"),
        P(("front", "row"), None),
        P(("front", "row")),
    )
    return jax.shard_map(
        body, mesh=mesh, in_specs=placed, out_specs=P("front", "row", "col"), check_vma=False
    )
```

```python
import functools
import jax
import jax.numpy as jnp
from jax import lax
from jax.experimental import pallas as pl
from jax.experimental.pallas import tpu as pltpu
from jax.sharding import PartitionSpec as P

PANEL_COLUMNS = 512
PANEL_COUNT = 2
STAIR_BLK = 128
STAIRS = 8
BLOCK = 128
HALF = 64
TILE = 256
PIECE = 64
LATE = 2
CHUNK = 512
TN = (((0,), (0,)), ((), ()))
NN = (((1,), (0,)), ((), ()))
MESH = pl.DeviceIdType.MESH


def split(x):
    hi = x.astype(jnp.bfloat16)
    return hi, (x - hi.astype(jnp.float32)).astype(jnp.bfloat16)


def dot(a, b, dims):
    return lax.dot_general(a, b, dims, preferred_element_type=jnp.float32)


def dot3(a, b, dims):
    a_hi, a_lo = a
    b_hi, b_lo = b
    return dot(a_lo, b_hi, dims) + dot(a_hi, b_lo, dims) + dot(a_hi, b_hi, dims)


def left_of(x, axis=0):
    hi, lo = split(x)
    return jnp.concatenate([lo, hi, hi], axis)


def right_of(x):
    hi, lo = split(x)
    return jnp.concatenate([hi, lo, hi], 0)


def shift_order(n):
    return sorted(range(1, n), key=lambda s: (-min(s, n - s), s))


def square_tiles(eliminated, n_col):
    tiles = eliminated // TILE
    packed = [(i, k) for i in range(tiles) for k in range(i, tiles)]
    return [packed[c::n_col] for c in range(n_col)]


def pick(col, values):
    out = values[0]
    for c in range(1, len(values)):
        out = jnp.where(col == c, values[c], out)
    return out


def remote(src, dst, send_sem, recv_sem, device):
    return pltpu.make_async_remote_copy(
        src_ref=src,
        dst_ref=dst,
        send_sem=send_sem,
        recv_sem=recv_sem,
        device_id=device,
        device_id_type=MESH,
    )


def front_kernel(
    n_front, n_row, n_col, cap, codes, own, child, out,
    prod, square, rows, pan, lhs, source, parcel,
    part, other, whole_sq, work, near, far, prev, late_pan,
    zs, zr, ys, yr, here_sem,
    s1, s2, s3, s4, s5, r1, r2, ro_s, ro_r, x_late, own_late, far_late,
):
    f = lax.axis_index("front")
    r = lax.axis_index("row")
    c = lax.axis_index("col")
    n_own, width = own.shape
    eliminated = pan.shape[1]
    order = [0] + shift_order(n_front)
    piece = min(PIECE, cap)
    per = cap // piece
    first = n_own + cap
    count = (n_front - 1) * per

    local = [
        pltpu.make_async_copy(child, source, here_sem.at[0]),
        pltpu.make_async_copy(own, rows.at[pl.ds(0, n_own)], here_sem.at[1]),
    ]
    for copy in local:
        copy.start()
    barrier = pltpu.get_barrier_semaphore()
    for s in range(1, n_front):
        pl.semaphore_signal(
            barrier, inc=1, device_id={"front": (f + s) % n_front}, device_id_type=MESH
        )
    for s in range(1, n_row):
        pl.semaphore_signal(
            barrier, inc=1, device_id={"row": (r + s) % n_row}, device_id_type=MESH
        )
    for s in range(1, n_col):
        pl.semaphore_signal(
            barrier, inc=1, device_id={"col": (c + s) % n_col}, device_id_type=MESH
        )
    pl.semaphore_wait(barrier, n_front + n_row + n_col - 3)

    def z_copy(j, target):
        return remote(
            parcel.at[pl.ds(pl.multiple_of(j * piece, piece), piece)],
            rows.at[pl.ds(pl.multiple_of(first + j * piece, piece), piece)],
            zs.at[j],
            zr.at[j],
            {"front": target},
        )

    groups = list(range(n_front - 1))
    even = sorted(groups, key=lambda q: (-min(order[1 + q], n_front - order[1 + q]), -q))

    def y_copy(slot, start, size, other):
        return remote(
            rows.at[pl.ds(start, size), pl.ds(0, eliminated)],
            pan.at[pl.ds(start, size)],
            ys.at[slot, other],
            yr.at[slot],
            {"col": other},
        )

    columns = c * width + lax.broadcasted_iota(jnp.int32, (1, width), 1)

    def pack(into, start, code_start, size):
        def one(i, carry):
            code = codes[code_start + i] - 1
            row = source[pl.ds(jnp.maximum(code, 0) // STAIRS, 1), :]
            edge = jnp.where(code < 0, n_col * width, code % STAIRS * STAIR_BLK)
            into[pl.ds(start + i, 1), :] = jnp.where(columns >= edge, row, 0.0)
            return carry

        lax.fori_loop(0, size, one, 0, unroll=4)

    local[0].wait()

    def post(j, carry):
        pack(parcel, j * piece, cap + j * piece, piece)
        z_copy(j, (f + pick(j // per, order[1:])) % n_front).start()
        return carry

    lax.fori_loop(0, count, post, 0)
    pack(rows, n_own, 0, cap)

    prod[...] = jnp.zeros_like(prod)
    square[...] = jnp.zeros_like(square)
    lists = square_tiles(eliminated, n_col)
    slots = len(lists[0])

    def panel(slot, start, size):
        @pl.when(c == 0)
        def _():
            for other in range(1, n_col):
                y_copy(slot, start, size, other).start()
            lhs[pl.ds(0, 3 * size)] = left_of(rows[pl.ds(start, size), pl.ds(0, eliminated)])

        @pl.when(c > 0)
        def _():
            y_copy(slot, start, size, 1).wait_recv()
            lhs[pl.ds(0, 3 * size)] = left_of(pan[pl.ds(start, size)])

    def products(start, size):
        def column(n, carry):
            at = pl.ds(pl.multiple_of(n * TILE, TILE), TILE)
            rhs = right_of(rows[pl.ds(start, size), at])
            for i in range(eliminated // TILE):
                tile = pl.ds(i * TILE, TILE)
                prod[tile, at] += dot(lhs[pl.ds(0, 3 * size), tile], rhs, TN)
            return carry

        lax.fori_loop(0, width // TILE, column, 0)

    def square_dot(a, b, size):
        row = pl.ds(pl.multiple_of(a * TILE, TILE), TILE)
        col = pl.ds(pl.multiple_of(b * TILE, TILE), TILE)
        lo, hi = lhs[pl.ds(0, size), col], lhs[pl.ds(size, size), col]
        return dot(lhs[pl.ds(0, 3 * size), row], jnp.concatenate([hi, lo, hi], 0), TN)

    def consume(slot, start, size):
        panel(slot, start, size)
        products(start, size)
        for j in range(slots):
            a = pick(c, [t[min(j, len(t) - 1)][0] for t in lists])
            b = pick(c, [t[min(j, len(t) - 1)][1] for t in lists])
            square[j] += square_dot(a, b, size)

    local[1].wait()
    consume(0, 0, n_own)
    consume(1, n_own, cap)

    def place(i):
        group = jnp.where(f % 2 == 1, i // per, pick(i // per, even))
        return group * per + i % per

    def arrived(i, carry):
        j = place(i)
        z_copy(j, f).wait_recv()
        consume(2 + j, pl.multiple_of(first + j * piece, piece), piece)
        return carry

    lax.fori_loop(0, count - LATE, arrived, 0)
    share = width // n_row
    low = r % 2
    high = r // 2
    mate = r + 1 - 2 * low
    across = r + 2 - 4 * high
    y = n_col - 1 - c
    steps = eliminated // BLOCK
    owner_rows = eliminated // n_row
    half = TILE // 2

    kept = pl.ds(pl.multiple_of(low * half, half), half)
    given = pl.ds(pl.multiple_of((1 - low) * half, half), half)

    def core_copy(j):
        return remote(square.at[j, given], part.at[j], s1.at[0, j], s1.at[1, j], {"row": mate})

    def x_copy(j):
        return remote(part.at[slots + j], other.at[j], s2.at[0, j], s2.at[1, j], {"row": across})

    def flip_copy(j, col):
        tile = whole_sq.at[n_col * j + col, kept]
        return remote(tile, tile, s3.at[0, j], s3.at[1, j], {"col": y})

    def flip_recv(j):
        tile = whole_sq.at[n_col * j + y, kept]
        return remote(tile, tile, s3.at[0, j], s3.at[1, j], {"col": y})

    def mate_copy(j, col, sems):
        tile = whole_sq.at[n_col * j + col, kept]
        return remote(tile, tile, sems.at[0, j], sems.at[1, j], {"row": mate})

    def mate_recv(j, col, sems):
        tile = whole_sq.at[n_col * j + col, given]
        return remote(tile, tile, sems.at[0, j], sems.at[1, j], {"row": mate})

    def near_copy(q, k):
        at = pl.ds(pl.multiple_of(k * BLOCK, BLOCK), BLOCK)
        cols = pl.ds(pl.multiple_of((2 * q + 1 - low) * share, share), share)
        return remote(prod.at[at, cols], near.at[q, at], r1.at[0, q, k], r1.at[1, q, k], {"row": mate})

    theirs = pl.ds(pl.multiple_of((2 * (1 - high) + low) * share, share), share)
    ours = pl.ds(pl.multiple_of((2 * high + low) * share, share), share)

    def far_copy(k):
        at = pl.ds(pl.multiple_of(k * BLOCK, BLOCK), BLOCK)
        return remote(prod.at[at, theirs], far.at[at], r2.at[0, k], r2.at[1, k], {"row": across})

    def late_start(h):
        return pl.multiple_of(first + place(count - LATE + h) * piece, piece)

    def spread(h, source, device, sems):
        return remote(
            source,
            late_pan.at[r, pl.ds(h * piece, piece)],
            sems.at[0, h],
            sems.at[1, h],
            {"row": device},
        )

    def relay(h):
        there = late_pan.at[across, pl.ds(h * piece, piece)]
        return remote(there, there, far_late.at[0, h], far_late.at[1, h], {"row": mate})

    def received(h, source, sems):
        there = late_pan.at[source, pl.ds(h * piece, piece)]
        return remote(there, there, sems.at[0, h], sems.at[1, h], {"row": mate})

    def take(h):
        start = late_start(h)
        j = place(count - LATE + h)
        z_copy(j, f).wait_recv()
        panel(2 + j, start, piece)
        mine = pl.ds(h * piece, piece)

        @pl.when(c == 0)
        def _():
            there = rows.at[pl.ds(start, piece), pl.ds(0, eliminated)]
            spread(h, there, across, x_late).start()
            spread(h, there, mate, own_late).start()
            late_pan[r, mine] = rows[pl.ds(start, piece), pl.ds(0, eliminated)]

        @pl.when(c > 0)
        def _():
            there = pan.at[pl.ds(start, piece)]
            spread(h, there, across, x_late).start()
            spread(h, there, mate, own_late).start()
            late_pan[r, mine] = pan[pl.ds(start, piece)]

        products(start, piece)

    def late_square(h, add):
        received(h, mate, own_late).wait_recv()
        received(h, n_row - 1 - r, far_late).wait_recv()
        size = n_row * piece
        for q in range(n_row):
            hi, lo = split(late_pan[q, pl.ds(h * piece, piece)])
            lhs[pl.ds(q * piece, piece)] = lo
            lhs[pl.ds(size + q * piece, piece)] = hi
            lhs[pl.ds(2 * size + q * piece, piece)] = hi
        for col in range(n_col):
            for j, (a, b) in enumerate(lists[col]):
                tile = slice(a * TILE, (a + 1) * TILE), slice(b * TILE, (b + 1) * TILE)
                value = square_dot(a, b, size)
                if add:
                    value = value + work[tile]
                if h == LATE - 1:
                    value = value + whole_sq[n_col * j + col]
                work[tile] = value

    for j in range(slots):
        core_copy(j).start()
    for j in range(slots):
        core_copy(j).wait_recv()
        part[slots + j] = square[j, kept] + part[j]
        x_copy(j).start()
    for h in range(LATE - 1):
        take(h)
        if h == 0:
            for j in range(slots):
                x_copy(j).wait_recv()
                whole_sq[n_col * j + c, kept] = part[slots + j] + other[j]
                flip_copy(j, c).start()
                mate_copy(j, c, s4).start()
        received(h, across, x_late).wait_recv()
        relay(h).start()
        late_square(h, h > 0)
    take(LATE - 1)

    def hand(k, carry):
        for q in range(n_row // 2):
            near_copy(q, k).start()
        return carry

    lax.fori_loop(0, steps, hand, 0)
    for j in range(slots):
        flip_recv(j).wait_recv()
        mate_copy(j, y, s5).start()
    received(LATE - 1, across, x_late).wait_recv()
    relay(LATE - 1).start()
    for j in range(slots):
        mate_recv(j, c, s4).wait_recv()
        mate_recv(j, y, s5).wait_recv()
    late_square(LATE - 1, LATE > 1)

    def gather(k, carry):
        at = pl.ds(pl.multiple_of(k * BLOCK, BLOCK), BLOCK)
        for q in range(n_row // 2):
            near_copy(q, k).wait_recv()
        prod[at, theirs] += near[1 - high, at]
        far_copy(k).start()
        work[at, pl.ds(eliminated, share)] = prod[at, ours] + near[high, at]
        return carry

    lax.fori_loop(0, steps, gather, 0)

    def result_copy(k):
        at = pl.ds(pl.multiple_of(k * BLOCK, BLOCK), BLOCK)
        owner = k * BLOCK // owner_rows
        inside = pl.ds(pl.multiple_of(k * BLOCK % owner_rows, BLOCK), BLOCK)
        cols = pl.ds(pl.multiple_of(r * share, share), share)
        return remote(
            work.at[at, pl.ds(eliminated, share)],
            out.at[inside, cols],
            ro_s.at[k],
            ro_r.at[r, k % (owner_rows // BLOCK)],
            {"row": owner},
        )

    def result_recv(source, k):
        inside = pl.ds(k * BLOCK, BLOCK)
        cols = pl.ds(pl.multiple_of(source * share, share), share)
        return remote(
            work.at[inside, pl.ds(eliminated, share)],
            out.at[inside, cols],
            ro_s.at[k],
            ro_r.at[source, k],
            {"row": source},
        )

    def deliver(k):
        at = pl.ds(pl.multiple_of(k * BLOCK, BLOCK), BLOCK)
        owner = k * BLOCK // owner_rows

        @pl.when(owner == r)
        def _():
            inside = pl.ds(pl.multiple_of(k * BLOCK % owner_rows, BLOCK), BLOCK)
            out[inside, pl.ds(pl.multiple_of(r * share, share), share)] = work[at, eliminated:]

        @pl.when(owner != r)
        def _():
            result_copy(k).start()

    lanes = lax.broadcasted_iota(jnp.int32, (BLOCK, eliminated), 1)
    total = eliminated + share

    def outer(k, carry):
        at = pl.ds(pl.multiple_of(k * BLOCK, BLOCK), BLOCK)
        scale = left_of(block_inverse(work[at, at]), 1)
        far_copy(k).wait_recv()
        result = dot(scale, right_of(work[at, eliminated:] + far[at]), NN)
        work[at, eliminated:] = result
        prev[:, eliminated:] = right_of(result)
        top = dot(scale, right_of(work[at, :eliminated]), NN)
        top = jnp.where(lanes >= (k + 1) * BLOCK, top, 0.0)
        prev[:, :eliminated] = right_of(top)
        deliver(k)

        def inner(j, carry):
            rows = pl.ds(pl.multiple_of(j * BLOCK, BLOCK), BLOCK)
            hi, lo = prev[:BLOCK, rows], prev[BLOCK : 2 * BLOCK, rows]
            left = jnp.concatenate([lo, hi, hi], 0)
            for start in range(0, total, CHUNK):
                cols = slice(start, min(total, start + CHUNK))

                @pl.when(j * BLOCK < cols.stop)
                def _():
                    work[rows, cols] -= dot(left, prev[:, cols], TN)

            return carry

        lax.fori_loop(k + 1, steps, inner, 0)
        return carry

    lax.fori_loop(0, steps, outer, 0)

    for s in range(1, n_row):
        for k in range(owner_rows // BLOCK):
            result_recv((r + s) % n_row, k).wait_recv()

    def sent(k, carry):
        far_copy(k).wait_send()

        @pl.when(k * BLOCK // owner_rows != r)
        def _():
            result_copy(k).wait_send()

        return carry

    lax.fori_loop(0, steps, sent, 0)
    for j in range(slots):
        core_copy(j).wait_send()
        x_copy(j).wait_send()
        flip_copy(j, c).wait_send()
        mate_copy(j, c, s4).wait_send()
        mate_copy(j, y, s5).wait_send()
    for h in range(LATE):
        received(h, across, x_late).wait_send()
        received(h, mate, own_late).wait_send()
        relay(h).wait_send()

    def handed(k, carry):
        for q in range(n_row // 2):
            near_copy(q, k).wait_send()
        return carry

    lax.fori_loop(0, steps, handed, 0)

    @pl.when(c == 0)
    def _():
        for other in range(1, n_col):
            y_copy(0, 0, n_own, other).wait_send()
            y_copy(1, n_own, cap, other).wait_send()

            def sent(j, carry):
                start = pl.multiple_of(first + j * piece, piece)
                y_copy(2 + j, start, piece, other).wait_send()
                return carry

            lax.fori_loop(0, count, sent, 0)

    def left(j, carry):
        z_copy(j, f).wait_send()
        return carry

    lax.fori_loop(0, count, left, 0)


def small_inverse(block):
    lanes = lax.broadcasted_iota(jnp.int32, (HALF, HALF), 1)
    rows = lax.broadcasted_iota(jnp.int32, (HALF, HALF), 0)
    eye = (lanes == rows).astype(jnp.float32)
    both = jnp.concatenate([block, eye], 1)
    count = HALF // 8
    groups = [both[g * 8 : (g + 1) * 8] for g in range(count)]
    sub = lax.broadcasted_iota(jnp.int32, (8, 2 * HALF), 0)

    def column_of(g, j):
        return jnp.broadcast_to(groups[g][:, j : j + 1], (8, 2 * HALF))

    def row_of(x, s):
        return jnp.broadcast_to(x[s : s + 1], x.shape)

    for home in range(count):
        first = home * 8
        below = [[column_of(g, first + s) for s in range(8)] for g in range(home + 1, count)]
        columns = [column_of(home, first + s) for s in range(8)]
        solved = forward = groups[home]
        pivot = row_of(columns[0], 0)
        pivots = pivot
        for s in range(8):
            column = columns[s]
            inverse = 1.0 / pivot
            pivots = jnp.where(sub == s, pivot, pivots)
            forward = jnp.where(
                sub > s, forward - column * (row_of(forward, s) * inverse), forward
            )
            scaled = row_of(solved, s) * inverse
            solved = jnp.where(sub == s, scaled, solved - column * scaled)
            for t in range(s + 1, 8):
                row = row_of(columns[t], s)
                fresh = columns[t] - (column * row) * inverse
                if t == s + 1:
                    pivot = row_of(fresh, t)
                columns[t] = jnp.where(sub == s, row * inverse, fresh)
        groups[home] = forward * lax.rsqrt(pivots)
        spread = [row_of(solved, s) for s in range(8)]
        for g in range(home + 1, count):
            terms = [below[g - home - 1][s] * spread[s] for s in range(8)]
            while len(terms) > 1:
                terms = [terms[i] + terms[i + 1] for i in range(0, len(terms), 2)]
            groups[g] = groups[g] - terms[0]
    return jnp.concatenate(groups, 0)[:, HALF:]


def block_inverse(d):
    first = small_inverse(d[:HALF, :HALF])
    first_parts = split(first)
    r12 = dot3(first_parts, split(d[:HALF, HALF:]), NN)
    r12_parts = split(r12)
    second = small_inverse(d[HALF:, HALF:] - dot3(r12_parts, r12_parts, TN))
    corner = -dot3(split(second), split(dot3(r12_parts, first_parts, TN)), NN)
    return jnp.concatenate(
        [
            jnp.concatenate([first, jnp.zeros((HALF, HALF), jnp.float32)], 1),
            jnp.concatenate([corner, second], 1),
        ],
        0,
    )


def factor(codes, own, child, n_front, n_row, n_col, cap, eliminated):
    n_own, width = own.shape
    total = n_own + n_front * cap
    piece = min(PIECE, cap)
    count = (n_front - 1) * (cap // piece)
    slots = len(square_tiles(eliminated, n_col)[0])
    most = max(n_own, cap, n_row * piece)
    share = width // n_row
    steps = eliminated // BLOCK
    owner_rows = eliminated // n_row
    half = TILE // 2
    dma = pltpu.SemaphoreType.DMA
    f32 = jnp.float32
    return pl.pallas_call(
        functools.partial(front_kernel, n_front, n_row, n_col, cap),
        out_shape=jax.ShapeDtypeStruct((owner_rows, width), f32),
        in_specs=[pl.BlockSpec(memory_space=pltpu.SMEM)] + [pl.BlockSpec(memory_space=pl.ANY)] * 2,
        out_specs=pl.BlockSpec(memory_space=pltpu.VMEM),
        scratch_shapes=[
            pltpu.VMEM((eliminated, width), f32),
            pltpu.VMEM((slots, TILE, TILE), f32),
            pltpu.VMEM((total, width), f32),
            pltpu.VMEM((total, eliminated), f32),
            pltpu.VMEM((3 * most, eliminated), jnp.bfloat16),
            pltpu.VMEM(child.shape, f32),
            pltpu.VMEM((count * piece, width), f32),
            pltpu.VMEM((2 * slots, half, TILE), f32),
            pltpu.VMEM((slots, half, TILE), f32),
            pltpu.VMEM((n_col * slots, TILE, TILE), f32),
            pltpu.VMEM((eliminated, eliminated + share), f32),
            pltpu.VMEM((n_row // 2, eliminated, share), f32),
            pltpu.VMEM((eliminated, share), f32),
            pltpu.VMEM((3 * BLOCK, eliminated + share), jnp.bfloat16),
            pltpu.VMEM((n_row, LATE * piece, eliminated), f32),
            dma((count,)),
            dma((count,)),
            dma((count + 2, n_col)),
            dma((count + 2,)),
            dma((2,)),
            dma((2, slots)),
            dma((2, slots)),
            dma((2, slots)),
            dma((2, slots)),
            dma((2, slots)),
            dma((2, n_row // 2, steps)),
            dma((2, steps)),
            dma((steps,)),
            dma((n_row, owner_rows // BLOCK)),
            dma((2, LATE)),
            dma((2, LATE)),
            dma((2, LATE)),
        ],
        compiler_params=pltpu.CompilerParams(
            collective_id=0, has_side_effects=True, vmem_limit_bytes=67043328
        ),
    )(codes, own, child)


def body(own_rows, child_rows, child_dest, child_stair):
    n_front = lax.axis_size("front")
    n_row = lax.axis_size("row")
    n_col = lax.axis_size("col")
    source_rows = child_rows.shape[0]
    capacity = max(2, 2 * source_rows // n_front)
    targets = child_dest[:, 0]
    index = lax.iota(jnp.int32, source_rows)
    ahead = (targets[None, :] == targets[:, None]) & (index[None, :] < index[:, None])
    slot = jnp.sum(ahead.astype(jnp.int32), axis=1)
    shift = (targets - lax.axis_index("front")) % n_front
    rank = jnp.zeros_like(shift)
    for place, s in enumerate(shift_order(n_front)):
        rank = jnp.where(shift == s, place + 1, rank)
    position = rank * capacity + slot
    code = index * STAIRS + child_stair + 1
    places = lax.iota(jnp.int32, n_front * capacity)
    codes = jnp.sum(jnp.where(position[None, :] == places[:, None], code[None, :], 0), axis=1)
    eliminated = PANEL_COUNT * PANEL_COLUMNS
    result = factor(
        codes, own_rows[0], child_rows, n_front, n_row, n_col, capacity, eliminated
    )
    return result[None]


def solution(mesh):
    placed = (
        P("front", "row", "col"),
        P(("front", "row"), "col"),
        P(("front", "row"), None),
        P(("front", "row")),
    )
    return jax.shard_map(
        body, mesh=mesh, in_specs=placed, out_specs=P("front", "row", "col"), check_vma=False
    )
```

```python
import functools
import jax
import jax.numpy as jnp
from jax import lax
from jax.experimental import pallas as pl
from jax.experimental.pallas import tpu as pltpu
from jax.sharding import PartitionSpec as P

PANEL_COLUMNS = 512
PANEL_COUNT = 2
STAIR_BLK = 128
STAIRS = 8
BLOCK = 128
HALF = 64
TILE = 256
PIECE = 64
LATE = 2
CHUNK = 512
TN = (((0,), (0,)), ((), ()))
NN = (((1,), (0,)), ((), ()))
MESH = pl.DeviceIdType.MESH


def split(x):
    hi = x.astype(jnp.bfloat16)
    return hi, (x - hi.astype(jnp.float32)).astype(jnp.bfloat16)


def dot(a, b, dims):
    return lax.dot_general(a, b, dims, preferred_element_type=jnp.float32)


def dot3(a, b, dims):
    a_hi, a_lo = a
    b_hi, b_lo = b
    return dot(a_lo, b_hi, dims) + dot(a_hi, b_lo, dims) + dot(a_hi, b_hi, dims)


def left_of(x, axis=0):
    hi, lo = split(x)
    return jnp.concatenate([lo, hi, hi], axis)


def right_of(x):
    hi, lo = split(x)
    return jnp.concatenate([hi, lo, hi], 0)


def shift_order(n):
    return sorted(range(1, n), key=lambda s: (-min(s, n - s), s))


def send_order(f, n):
    up, down = list(range(n - 1, f, -1)), list(range(f))
    return down + up if 2 * f < n else up[::-1] + down


def arrival(f, g, n):
    place = send_order(f, n).index(g)
    depth = min(f, n - 1 - f)
    return place + (depth if place >= depth else 0)


def group_tables(n):
    group = {s: q for q, s in enumerate(shift_order(n))}
    sends, takes = [], []
    for f in range(n):
        sends += [group[(g - f) % n] for g in send_order(f, n)]
        sources = [g for g in range(n) if g != f]
        sources.sort(key=lambda g: arrival(g, f, n))
        takes += [group[(f - g) % n] for g in sources]
    return sends, takes


def square_tiles(eliminated, n_col):
    tiles = eliminated // TILE
    packed = [(i, k) for i in range(tiles) for k in range(i, tiles)]
    return [packed[c::n_col] for c in range(n_col)]


def pick(col, values):
    out = values[0]
    for c in range(1, len(values)):
        out = jnp.where(col == c, values[c], out)
    return out


def remote(src, dst, send_sem, recv_sem, device):
    return pltpu.make_async_remote_copy(
        src_ref=src,
        dst_ref=dst,
        send_sem=send_sem,
        recv_sem=recv_sem,
        device_id=device,
        device_id_type=MESH,
    )


def front_kernel(
    n_front, n_row, n_col, cap, codes, own, child, out,
    prod, square, rows, pan, lhs, source, parcel,
    part, other, whole_sq, work, near, far, prev, late_pan,
    zs, zr, ys, yr, here_sem,
    s1, s2, s3, s4, s5, r1, r2, ro_s, ro_r, x_late, own_late, far_late,
):
    f = lax.axis_index("front")
    r = lax.axis_index("row")
    c = lax.axis_index("col")
    n_own, width = own.shape
    eliminated = pan.shape[1]
    order = [0] + shift_order(n_front)
    piece = min(PIECE, cap)
    per = cap // piece
    first = n_own + cap
    count = (n_front - 1) * per

    local = [
        pltpu.make_async_copy(child, source, here_sem.at[0]),
        pltpu.make_async_copy(own, rows.at[pl.ds(0, n_own)], here_sem.at[1]),
    ]
    for copy in local:
        copy.start()
    barrier = pltpu.get_barrier_semaphore()
    for s in range(1, n_front):
        pl.semaphore_signal(
            barrier, inc=1, device_id={"front": (f + s) % n_front}, device_id_type=MESH
        )
    for s in range(1, n_row):
        pl.semaphore_signal(
            barrier, inc=1, device_id={"row": (r + s) % n_row}, device_id_type=MESH
        )
    for s in range(1, n_col):
        pl.semaphore_signal(
            barrier, inc=1, device_id={"col": (c + s) % n_col}, device_id_type=MESH
        )
    pl.semaphore_wait(barrier, n_front + n_row + n_col - 3)

    def z_copy(j, target):
        return remote(
            parcel.at[pl.ds(pl.multiple_of(j * piece, piece), piece)],
            rows.at[pl.ds(pl.multiple_of(first + j * piece, piece), piece)],
            zs.at[j],
            zr.at[j],
            {"front": target},
        )

    sends, takes = group_tables(n_front)

    def y_copy(slot, start, size, other):
        return remote(
            rows.at[pl.ds(start, size), pl.ds(0, eliminated)],
            pan.at[pl.ds(start, size)],
            ys.at[slot, other],
            yr.at[slot],
            {"col": other},
        )

    columns = c * width + lax.broadcasted_iota(jnp.int32, (1, width), 1)

    def pack(into, start, code_start, size):
        def one(i, carry):
            code = codes[code_start + i] - 1
            row = source[pl.ds(jnp.maximum(code, 0) // STAIRS, 1), :]
            edge = jnp.where(code < 0, n_col * width, code % STAIRS * STAIR_BLK)
            into[pl.ds(start + i, 1), :] = jnp.where(columns >= edge, row, 0.0)
            return carry

        lax.fori_loop(0, size, one, 0, unroll=4)

    local[0].wait()

    def post(i, carry):
        j = pick(f * (n_front - 1) + i // per, sends) * per + i % per
        pack(parcel, j * piece, cap + j * piece, piece)
        z_copy(j, (f + pick(j // per, order[1:])) % n_front).start()
        return carry

    lax.fori_loop(0, count, post, 0)
    pack(rows, n_own, 0, cap)

    prod[...] = jnp.zeros_like(prod)
    square[...] = jnp.zeros_like(square)
    lists = square_tiles(eliminated, n_col)
    slots = len(lists[0])

    def panel(slot, start, size):
        @pl.when(c == 0)
        def _():
            for other in range(1, n_col):
                y_copy(slot, start, size, other).start()
            lhs[pl.ds(0, 3 * size)] = left_of(rows[pl.ds(start, size), pl.ds(0, eliminated)])

        @pl.when(c > 0)
        def _():
            y_copy(slot, start, size, 1).wait_recv()
            lhs[pl.ds(0, 3 * size)] = left_of(pan[pl.ds(start, size)])

    def products(start, size):
        def column(n, carry):
            at = pl.ds(pl.multiple_of(n * TILE, TILE), TILE)
            rhs = right_of(rows[pl.ds(start, size), at])
            for i in range(eliminated // TILE):
                tile = pl.ds(i * TILE, TILE)
                prod[tile, at] += dot(lhs[pl.ds(0, 3 * size), tile], rhs, TN)
            return carry

        lax.fori_loop(0, width // TILE, column, 0)

    def square_dot(a, b, size):
        row = pl.ds(pl.multiple_of(a * TILE, TILE), TILE)
        col = pl.ds(pl.multiple_of(b * TILE, TILE), TILE)
        lo, hi = lhs[pl.ds(0, size), col], lhs[pl.ds(size, size), col]
        return dot(lhs[pl.ds(0, 3 * size), row], jnp.concatenate([hi, lo, hi], 0), TN)

    def consume(slot, start, size):
        panel(slot, start, size)
        products(start, size)
        for j in range(slots):
            a = pick(c, [t[min(j, len(t) - 1)][0] for t in lists])
            b = pick(c, [t[min(j, len(t) - 1)][1] for t in lists])
            square[j] += square_dot(a, b, size)

    local[1].wait()
    consume(0, 0, n_own)
    consume(1, n_own, cap)

    def place(i):
        group = pick(f * (n_front - 1) + i // per, takes)
        return group * per + i % per

    def arrived(i, carry):
        j = place(i)
        z_copy(j, f).wait_recv()
        consume(2 + j, pl.multiple_of(first + j * piece, piece), piece)
        return carry

    lax.fori_loop(0, count - LATE, arrived, 0)
    share = width // n_row
    low = r % 2
    high = r // 2
    mate = r + 1 - 2 * low
    across = r + 2 - 4 * high
    y = n_col - 1 - c
    steps = eliminated // BLOCK
    owner_rows = eliminated // n_row
    half = TILE // 2

    kept = pl.ds(pl.multiple_of(low * half, half), half)
    given = pl.ds(pl.multiple_of((1 - low) * half, half), half)

    def core_copy(j):
        return remote(square.at[j, given], part.at[j], s1.at[0, j], s1.at[1, j], {"row": mate})

    def x_copy(j):
        return remote(part.at[slots + j], other.at[j], s2.at[0, j], s2.at[1, j], {"row": across})

    def flip_copy(j, col):
        tile = whole_sq.at[n_col * j + col, kept]
        return remote(tile, tile, s3.at[0, j], s3.at[1, j], {"col": y})

    def flip_recv(j):
        tile = whole_sq.at[n_col * j + y, kept]
        return remote(tile, tile, s3.at[0, j], s3.at[1, j], {"col": y})

    def mate_copy(j, col, sems):
        tile = whole_sq.at[n_col * j + col, kept]
        return remote(tile, tile, sems.at[0, j], sems.at[1, j], {"row": mate})

    def mate_recv(j, col, sems):
        tile = whole_sq.at[n_col * j + col, given]
        return remote(tile, tile, sems.at[0, j], sems.at[1, j], {"row": mate})

    def near_copy(q, k):
        at = pl.ds(pl.multiple_of(k * BLOCK, BLOCK), BLOCK)
        cols = pl.ds(pl.multiple_of((2 * q + 1 - low) * share, share), share)
        return remote(prod.at[at, cols], near.at[q, at], r1.at[0, q, k], r1.at[1, q, k], {"row": mate})

    theirs = pl.ds(pl.multiple_of((2 * (1 - high) + low) * share, share), share)
    ours = pl.ds(pl.multiple_of((2 * high + low) * share, share), share)

    def far_copy(k):
        at = pl.ds(pl.multiple_of(k * BLOCK, BLOCK), BLOCK)
        return remote(prod.at[at, theirs], far.at[at], r2.at[0, k], r2.at[1, k], {"row": across})

    def late_start(h):
        return pl.multiple_of(first + place(count - LATE + h) * piece, piece)

    def spread(h, source, device, sems):
        return remote(
            source,
            late_pan.at[r, pl.ds(h * piece, piece)],
            sems.at[0, h],
            sems.at[1, h],
            {"row": device},
        )

    def relay(h):
        there = late_pan.at[across, pl.ds(h * piece, piece)]
        return remote(there, there, far_late.at[0, h], far_late.at[1, h], {"row": mate})

    def received(h, source, sems):
        there = late_pan.at[source, pl.ds(h * piece, piece)]
        return remote(there, there, sems.at[0, h], sems.at[1, h], {"row": mate})

    def take(h):
        start = late_start(h)
        j = place(count - LATE + h)
        z_copy(j, f).wait_recv()
        panel(2 + j, start, piece)
        mine = pl.ds(h * piece, piece)

        @pl.when(c == 0)
        def _():
            there = rows.at[pl.ds(start, piece), pl.ds(0, eliminated)]
            spread(h, there, across, x_late).start()
            spread(h, there, mate, own_late).start()
            late_pan[r, mine] = rows[pl.ds(start, piece), pl.ds(0, eliminated)]

        @pl.when(c > 0)
        def _():
            there = pan.at[pl.ds(start, piece)]
            spread(h, there, across, x_late).start()
            spread(h, there, mate, own_late).start()
            late_pan[r, mine] = pan[pl.ds(start, piece)]

        products(start, piece)

    def late_square(h, add):
        received(h, mate, own_late).wait_recv()
        received(h, n_row - 1 - r, far_late).wait_recv()
        size = n_row * piece
        for q in range(n_row):
            hi, lo = split(late_pan[q, pl.ds(h * piece, piece)])
            lhs[pl.ds(q * piece, piece)] = lo
            lhs[pl.ds(size + q * piece, piece)] = hi
            lhs[pl.ds(2 * size + q * piece, piece)] = hi
        for col in range(n_col):
            for j, (a, b) in enumerate(lists[col]):
                tile = slice(a * TILE, (a + 1) * TILE), slice(b * TILE, (b + 1) * TILE)
                value = square_dot(a, b, size)
                if add:
                    value = value + work[tile]
                if h == LATE - 1:
                    value = value + whole_sq[n_col * j + col]
                work[tile] = value

    for j in range(slots):
        core_copy(j).start()
    for j in range(slots):
        core_copy(j).wait_recv()
        part[slots + j] = square[j, kept] + part[j]
        x_copy(j).start()
    for h in range(LATE - 1):
        take(h)
        if h == 0:
            for j in range(slots):
                x_copy(j).wait_recv()
                whole_sq[n_col * j + c, kept] = part[slots + j] + other[j]
                flip_copy(j, c).start()
                mate_copy(j, c, s4).start()
        received(h, across, x_late).wait_recv()
        relay(h).start()
        late_square(h, h > 0)
    take(LATE - 1)

    def hand(k, carry):
        for q in range(n_row // 2):
            near_copy(q, k).start()
        return carry

    lax.fori_loop(0, steps, hand, 0)
    for j in range(slots):
        flip_recv(j).wait_recv()
        mate_copy(j, y, s5).start()
    received(LATE - 1, across, x_late).wait_recv()
    relay(LATE - 1).start()
    for j in range(slots):
        mate_recv(j, c, s4).wait_recv()
        mate_recv(j, y, s5).wait_recv()
    late_square(LATE - 1, LATE > 1)

    def gather(k, carry):
        at = pl.ds(pl.multiple_of(k * BLOCK, BLOCK), BLOCK)
        for q in range(n_row // 2):
            near_copy(q, k).wait_recv()
        prod[at, theirs] += near[1 - high, at]
        far_copy(k).start()
        work[at, pl.ds(eliminated, share)] = prod[at, ours] + near[high, at]
        return carry

    lax.fori_loop(0, steps, gather, 0)

    def result_copy(k):
        at = pl.ds(pl.multiple_of(k * BLOCK, BLOCK), BLOCK)
        owner = k * BLOCK // owner_rows
        inside = pl.ds(pl.multiple_of(k * BLOCK % owner_rows, BLOCK), BLOCK)
        cols = pl.ds(pl.multiple_of(r * share, share), share)
        return remote(
            work.at[at, pl.ds(eliminated, share)],
            out.at[inside, cols],
            ro_s.at[k],
            ro_r.at[r, k % (owner_rows // BLOCK)],
            {"row": owner},
        )

    def result_recv(source, k):
        inside = pl.ds(k * BLOCK, BLOCK)
        cols = pl.ds(pl.multiple_of(source * share, share), share)
        return remote(
            work.at[inside, pl.ds(eliminated, share)],
            out.at[inside, cols],
            ro_s.at[k],
            ro_r.at[source, k],
            {"row": source},
        )

    def deliver(k):
        at = pl.ds(pl.multiple_of(k * BLOCK, BLOCK), BLOCK)
        owner = k * BLOCK // owner_rows

        @pl.when(owner == r)
        def _():
            inside = pl.ds(pl.multiple_of(k * BLOCK % owner_rows, BLOCK), BLOCK)
            out[inside, pl.ds(pl.multiple_of(r * share, share), share)] = work[at, eliminated:]

        @pl.when(owner != r)
        def _():
            result_copy(k).start()

    lanes = lax.broadcasted_iota(jnp.int32, (BLOCK, eliminated), 1)
    total = eliminated + share

    def outer(k, carry):
        at = pl.ds(pl.multiple_of(k * BLOCK, BLOCK), BLOCK)
        scale = left_of(block_inverse(work[at, at]), 1)
        far_copy(k).wait_recv()
        result = dot(scale, right_of(work[at, eliminated:] + far[at]), NN)
        work[at, eliminated:] = result
        prev[:, eliminated:] = right_of(result)
        top = dot(scale, right_of(work[at, :eliminated]), NN)
        top = jnp.where(lanes >= (k + 1) * BLOCK, top, 0.0)
        prev[:, :eliminated] = right_of(top)
        deliver(k)

        def inner(j, carry):
            rows = pl.ds(pl.multiple_of(j * BLOCK, BLOCK), BLOCK)
            hi, lo = prev[:BLOCK, rows], prev[BLOCK : 2 * BLOCK, rows]
            left = jnp.concatenate([lo, hi, hi], 0)
            for start in range(0, total, CHUNK):
                cols = slice(start, min(total, start + CHUNK))

                @pl.when(j * BLOCK < cols.stop)
                def _():
                    work[rows, cols] -= dot(left, prev[:, cols], TN)

            return carry

        lax.fori_loop(k + 1, steps, inner, 0)
        return carry

    lax.fori_loop(0, steps, outer, 0)

    for s in range(1, n_row):
        for k in range(owner_rows // BLOCK):
            result_recv((r + s) % n_row, k).wait_recv()

    def sent(k, carry):
        far_copy(k).wait_send()

        @pl.when(k * BLOCK // owner_rows != r)
        def _():
            result_copy(k).wait_send()

        return carry

    lax.fori_loop(0, steps, sent, 0)
    for j in range(slots):
        core_copy(j).wait_send()
        x_copy(j).wait_send()
        flip_copy(j, c).wait_send()
        mate_copy(j, c, s4).wait_send()
        mate_copy(j, y, s5).wait_send()
    for h in range(LATE):
        received(h, across, x_late).wait_send()
        received(h, mate, own_late).wait_send()
        relay(h).wait_send()

    def handed(k, carry):
        for q in range(n_row // 2):
            near_copy(q, k).wait_send()
        return carry

    lax.fori_loop(0, steps, handed, 0)

    @pl.when(c == 0)
    def _():
        for other in range(1, n_col):
            y_copy(0, 0, n_own, other).wait_send()
            y_copy(1, n_own, cap, other).wait_send()

            def sent(j, carry):
                start = pl.multiple_of(first + j * piece, piece)
                y_copy(2 + j, start, piece, other).wait_send()
                return carry

            lax.fori_loop(0, count, sent, 0)

    def left(j, carry):
        z_copy(j, f).wait_send()
        return carry

    lax.fori_loop(0, count, left, 0)


def small_inverse(block):
    lanes = lax.broadcasted_iota(jnp.int32, (HALF, HALF), 1)
    rows = lax.broadcasted_iota(jnp.int32, (HALF, HALF), 0)
    eye = (lanes == rows).astype(jnp.float32)
    both = jnp.concatenate([block, eye], 1)
    count = HALF // 8
    groups = [both[g * 8 : (g + 1) * 8] for g in range(count)]
    sub = lax.broadcasted_iota(jnp.int32, (8, 2 * HALF), 0)

    def column_of(g, j):
        return jnp.broadcast_to(groups[g][:, j : j + 1], (8, 2 * HALF))

    def row_of(x, s):
        return jnp.broadcast_to(x[s : s + 1], x.shape)

    for home in range(count):
        first = home * 8
        below = [[column_of(g, first + s) for s in range(8)] for g in range(home + 1, count)]
        columns = [column_of(home, first + s) for s in range(8)]
        solved = forward = groups[home]
        pivot = row_of(columns[0], 0)
        pivots = pivot
        for s in range(8):
            column = columns[s]
            inverse = 1.0 / pivot
            pivots = jnp.where(sub == s, pivot, pivots)
            forward = jnp.where(
                sub > s, forward - column * (row_of(forward, s) * inverse), forward
            )
            scaled = row_of(solved, s) * inverse
            solved = jnp.where(sub == s, scaled, solved - column * scaled)
            for t in range(s + 1, 8):
                row = row_of(columns[t], s)
                fresh = columns[t] - (column * row) * inverse
                if t == s + 1:
                    pivot = row_of(fresh, t)
                columns[t] = jnp.where(sub == s, row * inverse, fresh)
        groups[home] = forward * lax.rsqrt(pivots)
        spread = [row_of(solved, s) for s in range(8)]
        for g in range(home + 1, count):
            terms = [below[g - home - 1][s] * spread[s] for s in range(8)]
            while len(terms) > 1:
                terms = [terms[i] + terms[i + 1] for i in range(0, len(terms), 2)]
            groups[g] = groups[g] - terms[0]
    return jnp.concatenate(groups, 0)[:, HALF:]


def block_inverse(d):
    first = small_inverse(d[:HALF, :HALF])
    first_parts = split(first)
    r12 = dot3(first_parts, split(d[:HALF, HALF:]), NN)
    r12_parts = split(r12)
    second = small_inverse(d[HALF:, HALF:] - dot3(r12_parts, r12_parts, TN))
    corner = -dot3(split(second), split(dot3(r12_parts, first_parts, TN)), NN)
    return jnp.concatenate(
        [
            jnp.concatenate([first, jnp.zeros((HALF, HALF), jnp.float32)], 1),
            jnp.concatenate([corner, second], 1),
        ],
        0,
    )


def factor(codes, own, child, n_front, n_row, n_col, cap, eliminated):
    n_own, width = own.shape
    total = n_own + n_front * cap
    piece = min(PIECE, cap)
    count = (n_front - 1) * (cap // piece)
    slots = len(square_tiles(eliminated, n_col)[0])
    most = max(n_own, cap, n_row * piece)
    share = width // n_row
    steps = eliminated // BLOCK
    owner_rows = eliminated // n_row
    half = TILE // 2
    dma = pltpu.SemaphoreType.DMA
    f32 = jnp.float32
    return pl.pallas_call(
        functools.partial(front_kernel, n_front, n_row, n_col, cap),
        out_shape=jax.ShapeDtypeStruct((owner_rows, width), f32),
        in_specs=[pl.BlockSpec(memory_space=pltpu.SMEM)] + [pl.BlockSpec(memory_space=pl.ANY)] * 2,
        out_specs=pl.BlockSpec(memory_space=pltpu.VMEM),
        scratch_shapes=[
            pltpu.VMEM((eliminated, width), f32),
            pltpu.VMEM((slots, TILE, TILE), f32),
            pltpu.VMEM((total, width), f32),
            pltpu.VMEM((total, eliminated), f32),
            pltpu.VMEM((3 * most, eliminated), jnp.bfloat16),
            pltpu.VMEM(child.shape, f32),
            pltpu.VMEM((count * piece, width), f32),
            pltpu.VMEM((2 * slots, half, TILE), f32),
            pltpu.VMEM((slots, half, TILE), f32),
            pltpu.VMEM((n_col * slots, TILE, TILE), f32),
            pltpu.VMEM((eliminated, eliminated + share), f32),
            pltpu.VMEM((n_row // 2, eliminated, share), f32),
            pltpu.VMEM((eliminated, share), f32),
            pltpu.VMEM((3 * BLOCK, eliminated + share), jnp.bfloat16),
            pltpu.VMEM((n_row, LATE * piece, eliminated), f32),
            dma((count,)),
            dma((count,)),
            dma((count + 2, n_col)),
            dma((count + 2,)),
            dma((2,)),
            dma((2, slots)),
            dma((2, slots)),
            dma((2, slots)),
            dma((2, slots)),
            dma((2, slots)),
            dma((2, n_row // 2, steps)),
            dma((2, steps)),
            dma((steps,)),
            dma((n_row, owner_rows // BLOCK)),
            dma((2, LATE)),
            dma((2, LATE)),
            dma((2, LATE)),
        ],
        compiler_params=pltpu.CompilerParams(
            collective_id=0, has_side_effects=True, vmem_limit_bytes=67043328
        ),
    )(codes, own, child)


def body(own_rows, child_rows, child_dest, child_stair):
    n_front = lax.axis_size("front")
    n_row = lax.axis_size("row")
    n_col = lax.axis_size("col")
    source_rows = child_rows.shape[0]
    capacity = max(2, 2 * source_rows // n_front)
    targets = child_dest[:, 0]
    index = lax.iota(jnp.int32, source_rows)
    ahead = (targets[None, :] == targets[:, None]) & (index[None, :] < index[:, None])
    slot = jnp.sum(ahead.astype(jnp.int32), axis=1)
    shift = (targets - lax.axis_index("front")) % n_front
    rank = jnp.zeros_like(shift)
    for place, s in enumerate(shift_order(n_front)):
        rank = jnp.where(shift == s, place + 1, rank)
    position = rank * capacity + slot
    code = index * STAIRS + child_stair + 1
    places = lax.iota(jnp.int32, n_front * capacity)
    codes = jnp.sum(jnp.where(position[None, :] == places[:, None], code[None, :], 0), axis=1)
    eliminated = PANEL_COUNT * PANEL_COLUMNS
    result = factor(
        codes, own_rows[0], child_rows, n_front, n_row, n_col, capacity, eliminated
    )
    return result[None]


def solution(mesh):
    placed = (
        P("front", "row", "col"),
        P(("front", "row"), "col"),
        P(("front", "row"), None),
        P(("front", "row")),
    )
    return jax.shard_map(
        body, mesh=mesh, in_specs=placed, out_specs=P("front", "row", "col"), check_vma=False
    )
```

```python
import functools
import jax
import jax.numpy as jnp
from jax import lax
from jax.experimental import pallas as pl
from jax.experimental.pallas import tpu as pltpu
from jax.sharding import PartitionSpec as P

PANEL_COLUMNS = 512
PANEL_COUNT = 2
STAIR_BLK = 128
STAIRS = 8
BLOCK = 128
HALF = 64
TILE = 256
PIECE = 64
LATE = 2
AHEAD = 2
CHUNK = 512
TN = (((0,), (0,)), ((), ()))
NN = (((1,), (0,)), ((), ()))
MESH = pl.DeviceIdType.MESH


def split(x):
    hi = x.astype(jnp.bfloat16)
    return hi, (x - hi.astype(jnp.float32)).astype(jnp.bfloat16)


def dot(a, b, dims):
    return lax.dot_general(a, b, dims, preferred_element_type=jnp.float32)


def dot3(a, b, dims):
    a_hi, a_lo = a
    b_hi, b_lo = b
    return dot(a_lo, b_hi, dims) + dot(a_hi, b_lo, dims) + dot(a_hi, b_hi, dims)


def left_of(x, axis=0):
    hi, lo = split(x)
    return jnp.concatenate([lo, hi, hi], axis)


def right_of(x):
    hi, lo = split(x)
    return jnp.concatenate([hi, lo, hi], 0)


def shift_order(n):
    return sorted(range(1, n), key=lambda s: (-min(s, n - s), s))


def send_order(f, n):
    up, down = list(range(n - 1, f, -1)), list(range(f))
    return down + up if 2 * f < n else up[::-1] + down


def arrival(f, g, n):
    place = send_order(f, n).index(g)
    depth = min(f, n - 1 - f)
    return place + (depth if place >= depth else 0)


def group_tables(n):
    group = {s: q for q, s in enumerate(shift_order(n))}
    sends, takes = [], []
    for f in range(n):
        sends += [group[(g - f) % n] for g in send_order(f, n)]
        sources = [g for g in range(n) if g != f]
        sources.sort(key=lambda g: arrival(g, f, n))
        takes += [group[(f - g) % n] for g in sources]
    return sends, takes


def square_tiles(eliminated, n_col):
    tiles = eliminated // TILE
    packed = [(i, k) for i in range(tiles) for k in range(i, tiles)]
    return [packed[c::n_col] for c in range(n_col)]


def pick(col, values):
    out = values[0]
    for c in range(1, len(values)):
        out = jnp.where(col == c, values[c], out)
    return out


def remote(src, dst, send_sem, recv_sem, device):
    return pltpu.make_async_remote_copy(
        src_ref=src,
        dst_ref=dst,
        send_sem=send_sem,
        recv_sem=recv_sem,
        device_id=device,
        device_id_type=MESH,
    )


def front_kernel(
    n_front, n_row, n_col, cap, codes, own, child, out,
    prod, square, rows, pan, lhs, source, parcel,
    part, other, whole_sq, work, near, far, prev, late_pan,
    zs, zr, ys, yr, here_sem,
    s1, s2, s3, s4, s5, r1, r2, ro_s, ro_r, x_late, own_late, far_late,
):
    f = lax.axis_index("front")
    r = lax.axis_index("row")
    c = lax.axis_index("col")
    n_own, width = own.shape
    eliminated = pan.shape[1]
    order = [0] + shift_order(n_front)
    piece = min(PIECE, cap)
    per = cap // piece
    first = n_own + cap
    count = (n_front - 1) * per

    local = [
        pltpu.make_async_copy(child, source, here_sem.at[0]),
        pltpu.make_async_copy(own, rows.at[pl.ds(0, n_own)], here_sem.at[1]),
    ]
    for copy in local:
        copy.start()
    barrier = pltpu.get_barrier_semaphore()
    for s in range(1, n_front):
        pl.semaphore_signal(
            barrier, inc=1, device_id={"front": (f + s) % n_front}, device_id_type=MESH
        )
    for s in range(1, n_row):
        pl.semaphore_signal(
            barrier, inc=1, device_id={"row": (r + s) % n_row}, device_id_type=MESH
        )
    for s in range(1, n_col):
        pl.semaphore_signal(
            barrier, inc=1, device_id={"col": (c + s) % n_col}, device_id_type=MESH
        )
    pl.semaphore_wait(barrier, n_front + n_row + n_col - 3)

    def z_copy(j, target):
        return remote(
            parcel.at[pl.ds(pl.multiple_of(j * piece, piece), piece)],
            rows.at[pl.ds(pl.multiple_of(first + j * piece, piece), piece)],
            zs.at[j],
            zr.at[j],
            {"front": target},
        )

    sends, takes = group_tables(n_front)

    def y_copy(slot, start, size, other):
        return remote(
            rows.at[pl.ds(start, size), pl.ds(0, eliminated)],
            pan.at[pl.ds(start, size)],
            ys.at[slot, other],
            yr.at[slot],
            {"col": other},
        )

    columns = c * width + lax.broadcasted_iota(jnp.int32, (1, width), 1)

    def pack(into, start, code_start, size):
        def one(i, carry):
            code = codes[code_start + i] - 1
            row = source[pl.ds(jnp.maximum(code, 0) // STAIRS, 1), :]
            edge = jnp.where(code < 0, n_col * width, code % STAIRS * STAIR_BLK)
            into[pl.ds(start + i, 1), :] = jnp.where(columns >= edge, row, 0.0)
            return carry

        lax.fori_loop(0, size, one, 0, unroll=4)

    local[0].wait()

    def post(i, carry):
        j = pick(f * (n_front - 1) + i // per, sends) * per + i % per
        pack(parcel, j * piece, cap + j * piece, piece)
        z_copy(j, (f + pick(j // per, order[1:])) % n_front).start()
        return carry

    lax.fori_loop(0, count, post, 0)
    pack(rows, n_own, 0, cap)

    prod[...] = jnp.zeros_like(prod)
    square[...] = jnp.zeros_like(square)
    work[:, eliminated:] = jnp.zeros((eliminated, work.shape[1] - eliminated), jnp.float32)
    lists = square_tiles(eliminated, n_col)
    slots = len(lists[0])

    def panel(slot, start, size):
        @pl.when(c == 0)
        def _():
            for other in range(1, n_col):
                y_copy(slot, start, size, other).start()
            lhs[pl.ds(0, 3 * size)] = left_of(rows[pl.ds(start, size), pl.ds(0, eliminated)])

        @pl.when(c > 0)
        def _():
            y_copy(slot, start, size, 1).wait_recv()
            lhs[pl.ds(0, 3 * size)] = left_of(pan[pl.ds(start, size)])

    def products(start, size):
        def column(n, carry):
            at = pl.ds(pl.multiple_of(n * TILE, TILE), TILE)
            rhs = right_of(rows[pl.ds(start, size), at])
            for i in range(eliminated // TILE):
                tile = pl.ds(i * TILE, TILE)
                prod[tile, at] += dot(lhs[pl.ds(0, 3 * size), tile], rhs, TN)
            return carry

        lax.fori_loop(0, width // TILE, column, 0)

    def square_dot(a, b, size):
        row = pl.ds(pl.multiple_of(a * TILE, TILE), TILE)
        col = pl.ds(pl.multiple_of(b * TILE, TILE), TILE)
        lo, hi = lhs[pl.ds(0, size), col], lhs[pl.ds(size, size), col]
        return dot(lhs[pl.ds(0, 3 * size), row], jnp.concatenate([hi, lo, hi], 0), TN)

    def consume(slot, start, size):
        panel(slot, start, size)
        products(start, size)
        for j in range(slots):
            a = pick(c, [t[min(j, len(t) - 1)][0] for t in lists])
            b = pick(c, [t[min(j, len(t) - 1)][1] for t in lists])
            square[j] += square_dot(a, b, size)

    local[1].wait()
    consume(0, 0, n_own)
    consume(1, n_own, cap)

    def place(i):
        group = pick(f * (n_front - 1) + i // per, takes)
        return group * per + i % per

    def arrived(i, carry):
        j = place(i)
        z_copy(j, f).wait_recv()
        consume(2 + j, pl.multiple_of(first + j * piece, piece), piece)
        return carry

    lax.fori_loop(0, count - LATE, arrived, 0)
    share = width // n_row
    low = r % 2
    high = r // 2
    mate = r + 1 - 2 * low
    across = r + 2 - 4 * high
    y = n_col - 1 - c
    steps = eliminated // BLOCK
    owner_rows = eliminated // n_row
    half = TILE // 2

    kept = pl.ds(pl.multiple_of(low * half, half), half)
    given = pl.ds(pl.multiple_of((1 - low) * half, half), half)

    def core_copy(j):
        return remote(square.at[j, given], part.at[j], s1.at[0, j], s1.at[1, j], {"row": mate})

    def x_copy(j):
        return remote(part.at[slots + j], other.at[j], s2.at[0, j], s2.at[1, j], {"row": across})

    def flip_copy(j, col):
        tile = whole_sq.at[n_col * j + col, kept]
        return remote(tile, tile, s3.at[0, j], s3.at[1, j], {"col": y})

    def flip_recv(j):
        tile = whole_sq.at[n_col * j + y, kept]
        return remote(tile, tile, s3.at[0, j], s3.at[1, j], {"col": y})

    def mate_copy(j, col, sems):
        tile = whole_sq.at[n_col * j + col, kept]
        return remote(tile, tile, sems.at[0, j], sems.at[1, j], {"row": mate})

    def mate_recv(j, col, sems):
        tile = whole_sq.at[n_col * j + col, given]
        return remote(tile, tile, sems.at[0, j], sems.at[1, j], {"row": mate})

    def near_copy(q, k):
        at = pl.ds(pl.multiple_of(k * BLOCK, BLOCK), BLOCK)
        cols = pl.ds(pl.multiple_of((2 * q + 1 - low) * share, share), share)
        return remote(prod.at[at, cols], near.at[q, at], r1.at[0, q, k], r1.at[1, q, k], {"row": mate})

    theirs = pl.ds(pl.multiple_of((2 * (1 - high) + low) * share, share), share)
    ours = pl.ds(pl.multiple_of((2 * high + low) * share, share), share)

    def far_copy(k):
        at = pl.ds(pl.multiple_of(k * BLOCK, BLOCK), BLOCK)
        return remote(prod.at[at, theirs], far.at[at], r2.at[0, k], r2.at[1, k], {"row": across})

    def late_start(h):
        return pl.multiple_of(first + place(count - LATE + h) * piece, piece)

    def spread(h, source, device, sems):
        return remote(
            source,
            late_pan.at[r, pl.ds(h * piece, piece)],
            sems.at[0, h],
            sems.at[1, h],
            {"row": device},
        )

    def relay(h):
        there = late_pan.at[across, pl.ds(h * piece, piece)]
        return remote(there, there, far_late.at[0, h], far_late.at[1, h], {"row": mate})

    def received(h, source, sems):
        there = late_pan.at[source, pl.ds(h * piece, piece)]
        return remote(there, there, sems.at[0, h], sems.at[1, h], {"row": mate})

    def take(h):
        start = late_start(h)
        j = place(count - LATE + h)
        z_copy(j, f).wait_recv()
        panel(2 + j, start, piece)
        mine = pl.ds(h * piece, piece)

        @pl.when(c == 0)
        def _():
            there = rows.at[pl.ds(start, piece), pl.ds(0, eliminated)]
            spread(h, there, across, x_late).start()
            spread(h, there, mate, own_late).start()
            late_pan[r, mine] = rows[pl.ds(start, piece), pl.ds(0, eliminated)]

        @pl.when(c > 0)
        def _():
            there = pan.at[pl.ds(start, piece)]
            spread(h, there, across, x_late).start()
            spread(h, there, mate, own_late).start()
            late_pan[r, mine] = pan[pl.ds(start, piece)]

        products(start, piece)

    def late_square(h, add):
        received(h, mate, own_late).wait_recv()
        received(h, n_row - 1 - r, far_late).wait_recv()
        size = n_row * piece
        for q in range(n_row):
            hi, lo = split(late_pan[q, pl.ds(h * piece, piece)])
            lhs[pl.ds(q * piece, piece)] = lo
            lhs[pl.ds(size + q * piece, piece)] = hi
            lhs[pl.ds(2 * size + q * piece, piece)] = hi
        for col in range(n_col):
            for j, (a, b) in enumerate(lists[col]):
                tile = slice(a * TILE, (a + 1) * TILE), slice(b * TILE, (b + 1) * TILE)
                value = square_dot(a, b, size)
                if add:
                    value = value + work[tile]
                if h == LATE - 1:
                    value = value + whole_sq[n_col * j + col]
                work[tile] = value

    for j in range(slots):
        core_copy(j).start()
    for j in range(slots):
        core_copy(j).wait_recv()
        part[slots + j] = square[j, kept] + part[j]
        x_copy(j).start()
    for h in range(LATE - 1):
        take(h)
        if h == 0:
            for j in range(slots):
                x_copy(j).wait_recv()
                whole_sq[n_col * j + c, kept] = part[slots + j] + other[j]
                flip_copy(j, c).start()
                mate_copy(j, c, s4).start()
        received(h, across, x_late).wait_recv()
        relay(h).start()
        late_square(h, h > 0)
    take(LATE - 1)

    def hand(k, carry):
        for q in range(n_row // 2):
            near_copy(q, k).start()
        return carry

    lax.fori_loop(0, steps, hand, 0)
    for j in range(slots):
        flip_recv(j).wait_recv()
        mate_copy(j, y, s5).start()
    received(LATE - 1, across, x_late).wait_recv()
    relay(LATE - 1).start()
    for j in range(slots):
        mate_recv(j, c, s4).wait_recv()
        mate_recv(j, y, s5).wait_recv()
    late_square(LATE - 1, LATE > 1)

    def gather(k, carry):
        at = pl.ds(pl.multiple_of(k * BLOCK, BLOCK), BLOCK)
        for q in range(n_row // 2):
            near_copy(q, k).wait_recv()
        prod[at, theirs] += near[1 - high, at]
        far_copy(k).start()
        work[at, pl.ds(eliminated, share)] += prod[at, ours] + near[high, at]
        return carry

    lax.fori_loop(0, AHEAD, gather, 0)

    def result_copy(k):
        at = pl.ds(pl.multiple_of(k * BLOCK, BLOCK), BLOCK)
        owner = k * BLOCK // owner_rows
        inside = pl.ds(pl.multiple_of(k * BLOCK % owner_rows, BLOCK), BLOCK)
        cols = pl.ds(pl.multiple_of(r * share, share), share)
        return remote(
            work.at[at, pl.ds(eliminated, share)],
            out.at[inside, cols],
            ro_s.at[k],
            ro_r.at[r, k % (owner_rows // BLOCK)],
            {"row": owner},
        )

    def result_recv(source, k):
        inside = pl.ds(k * BLOCK, BLOCK)
        cols = pl.ds(pl.multiple_of(source * share, share), share)
        return remote(
            work.at[inside, pl.ds(eliminated, share)],
            out.at[inside, cols],
            ro_s.at[k],
            ro_r.at[source, k],
            {"row": source},
        )

    def deliver(k):
        at = pl.ds(pl.multiple_of(k * BLOCK, BLOCK), BLOCK)
        owner = k * BLOCK // owner_rows

        @pl.when(owner == r)
        def _():
            inside = pl.ds(pl.multiple_of(k * BLOCK % owner_rows, BLOCK), BLOCK)
            out[inside, pl.ds(pl.multiple_of(r * share, share), share)] = work[at, eliminated:]

        @pl.when(owner != r)
        def _():
            result_copy(k).start()

    lanes = lax.broadcasted_iota(jnp.int32, (BLOCK, eliminated), 1)
    total = eliminated + share

    def outer(k, carry):
        at = pl.ds(pl.multiple_of(k * BLOCK, BLOCK), BLOCK)
        lax.fori_loop(
            jnp.minimum(AHEAD * (k + 1), steps), jnp.minimum(AHEAD * (k + 2), steps), gather, 0
        )
        scale = left_of(block_inverse(work[at, at]), 1)
        far_copy(k).wait_recv()
        result = dot(scale, right_of(work[at, eliminated:] + far[at]), NN)
        work[at, eliminated:] = result
        prev[:, eliminated:] = right_of(result)
        top = dot(scale, right_of(work[at, :eliminated]), NN)
        top = jnp.where(lanes >= (k + 1) * BLOCK, top, 0.0)
        prev[:, :eliminated] = right_of(top)
        deliver(k)

        def inner(j, carry):
            rows = pl.ds(pl.multiple_of(j * BLOCK, BLOCK), BLOCK)
            hi, lo = prev[:BLOCK, rows], prev[BLOCK : 2 * BLOCK, rows]
            left = jnp.concatenate([lo, hi, hi], 0)
            for start in range(0, total, CHUNK):
                cols = slice(start, min(total, start + CHUNK))

                @pl.when(j * BLOCK < cols.stop)
                def _():
                    work[rows, cols] -= dot(left, prev[:, cols], TN)

            return carry

        lax.fori_loop(k + 1, steps, inner, 0)
        return carry

    lax.fori_loop(0, steps, outer, 0)

    for s in range(1, n_row):
        for k in range(owner_rows // BLOCK):
            result_recv((r + s) % n_row, k).wait_recv()

    def sent(k, carry):
        far_copy(k).wait_send()

        @pl.when(k * BLOCK // owner_rows != r)
        def _():
            result_copy(k).wait_send()

        return carry

    lax.fori_loop(0, steps, sent, 0)
    for j in range(slots):
        core_copy(j).wait_send()
        x_copy(j).wait_send()
        flip_copy(j, c).wait_send()
        mate_copy(j, c, s4).wait_send()
        mate_copy(j, y, s5).wait_send()
    for h in range(LATE):
        received(h, across, x_late).wait_send()
        received(h, mate, own_late).wait_send()
        relay(h).wait_send()

    def handed(k, carry):
        for q in range(n_row // 2):
            near_copy(q, k).wait_send()
        return carry

    lax.fori_loop(0, steps, handed, 0)

    @pl.when(c == 0)
    def _():
        for other in range(1, n_col):
            y_copy(0, 0, n_own, other).wait_send()
            y_copy(1, n_own, cap, other).wait_send()

            def sent(j, carry):
                start = pl.multiple_of(first + j * piece, piece)
                y_copy(2 + j, start, piece, other).wait_send()
                return carry

            lax.fori_loop(0, count, sent, 0)

    def left(j, carry):
        z_copy(j, f).wait_send()
        return carry

    lax.fori_loop(0, count, left, 0)


def small_inverse(block):
    lanes = lax.broadcasted_iota(jnp.int32, (HALF, HALF), 1)
    rows = lax.broadcasted_iota(jnp.int32, (HALF, HALF), 0)
    eye = (lanes == rows).astype(jnp.float32)
    both = jnp.concatenate([block, eye], 1)
    count = HALF // 8
    groups = [both[g * 8 : (g + 1) * 8] for g in range(count)]
    sub = lax.broadcasted_iota(jnp.int32, (8, 2 * HALF), 0)

    def column_of(g, j):
        return jnp.broadcast_to(groups[g][:, j : j + 1], (8, 2 * HALF))

    def row_of(x, s):
        return jnp.broadcast_to(x[s : s + 1], x.shape)

    for home in range(count):
        first = home * 8
        below = [[column_of(g, first + s) for s in range(8)] for g in range(home + 1, count)]
        columns = [column_of(home, first + s) for s in range(8)]
        solved = forward = groups[home]
        pivot = row_of(columns[0], 0)
        pivots = pivot
        for s in range(8):
            column = columns[s]
            inverse = 1.0 / pivot
            pivots = jnp.where(sub == s, pivot, pivots)
            forward = jnp.where(
                sub > s, forward - column * (row_of(forward, s) * inverse), forward
            )
            scaled = row_of(solved, s) * inverse
            solved = jnp.where(sub == s, scaled, solved - column * scaled)
            for t in range(s + 1, 8):
                row = row_of(columns[t], s)
                fresh = columns[t] - (column * row) * inverse
                if t == s + 1:
                    pivot = row_of(fresh, t)
                columns[t] = jnp.where(sub == s, row * inverse, fresh)
        groups[home] = forward * lax.rsqrt(pivots)
        spread = [row_of(solved, s) for s in range(8)]
        for g in range(home + 1, count):
            terms = [below[g - home - 1][s] * spread[s] for s in range(8)]
            while len(terms) > 1:
                terms = [terms[i] + terms[i + 1] for i in range(0, len(terms), 2)]
            groups[g] = groups[g] - terms[0]
    return jnp.concatenate(groups, 0)[:, HALF:]


def block_inverse(d):
    first = small_inverse(d[:HALF, :HALF])
    first_parts = split(first)
    r12 = dot3(first_parts, split(d[:HALF, HALF:]), NN)
    r12_parts = split(r12)
    second = small_inverse(d[HALF:, HALF:] - dot3(r12_parts, r12_parts, TN))
    corner = -dot3(split(second), split(dot3(r12_parts, first_parts, TN)), NN)
    return jnp.concatenate(
        [
            jnp.concatenate([first, jnp.zeros((HALF, HALF), jnp.float32)], 1),
            jnp.concatenate([corner, second], 1),
        ],
        0,
    )


def factor(codes, own, child, n_front, n_row, n_col, cap, eliminated):
    n_own, width = own.shape
    total = n_own + n_front * cap
    piece = min(PIECE, cap)
    count = (n_front - 1) * (cap // piece)
    slots = len(square_tiles(eliminated, n_col)[0])
    most = max(n_own, cap, n_row * piece)
    share = width // n_row
    steps = eliminated // BLOCK
    owner_rows = eliminated // n_row
    half = TILE // 2
    dma = pltpu.SemaphoreType.DMA
    f32 = jnp.float32
    return pl.pallas_call(
        functools.partial(front_kernel, n_front, n_row, n_col, cap),
        out_shape=jax.ShapeDtypeStruct((owner_rows, width), f32),
        in_specs=[pl.BlockSpec(memory_space=pltpu.SMEM)] + [pl.BlockSpec(memory_space=pl.ANY)] * 2,
        out_specs=pl.BlockSpec(memory_space=pltpu.VMEM),
        scratch_shapes=[
            pltpu.VMEM((eliminated, width), f32),
            pltpu.VMEM((slots, TILE, TILE), f32),
            pltpu.VMEM((total, width), f32),
            pltpu.VMEM((total, eliminated), f32),
            pltpu.VMEM((3 * most, eliminated), jnp.bfloat16),
            pltpu.VMEM(child.shape, f32),
            pltpu.VMEM((count * piece, width), f32),
            pltpu.VMEM((2 * slots, half, TILE), f32),
            pltpu.VMEM((slots, half, TILE), f32),
            pltpu.VMEM((n_col * slots, TILE, TILE), f32),
            pltpu.VMEM((eliminated, eliminated + share), f32),
            pltpu.VMEM((n_row // 2, eliminated, share), f32),
            pltpu.VMEM((eliminated, share), f32),
            pltpu.VMEM((3 * BLOCK, eliminated + share), jnp.bfloat16),
            pltpu.VMEM((n_row, LATE * piece, eliminated), f32),
            dma((count,)),
            dma((count,)),
            dma((count + 2, n_col)),
            dma((count + 2,)),
            dma((2,)),
            dma((2, slots)),
            dma((2, slots)),
            dma((2, slots)),
            dma((2, slots)),
            dma((2, slots)),
            dma((2, n_row // 2, steps)),
            dma((2, steps)),
            dma((steps,)),
            dma((n_row, owner_rows // BLOCK)),
            dma((2, LATE)),
            dma((2, LATE)),
            dma((2, LATE)),
        ],
        compiler_params=pltpu.CompilerParams(
            collective_id=0, has_side_effects=True, vmem_limit_bytes=67043328
        ),
    )(codes, own, child)


def body(own_rows, child_rows, child_dest, child_stair):
    n_front = lax.axis_size("front")
    n_row = lax.axis_size("row")
    n_col = lax.axis_size("col")
    source_rows = child_rows.shape[0]
    capacity = max(2, 2 * source_rows // n_front)
    targets = child_dest[:, 0]
    index = lax.iota(jnp.int32, source_rows)
    ahead = (targets[None, :] == targets[:, None]) & (index[None, :] < index[:, None])
    slot = jnp.sum(ahead.astype(jnp.int32), axis=1)
    shift = (targets - lax.axis_index("front")) % n_front
    rank = jnp.zeros_like(shift)
    for place, s in enumerate(shift_order(n_front)):
        rank = jnp.where(shift == s, place + 1, rank)
    position = rank * capacity + slot
    code = index * STAIRS + child_stair + 1
    places = lax.iota(jnp.int32, n_front * capacity)
    codes = jnp.sum(jnp.where(position[None, :] == places[:, None], code[None, :], 0), axis=1)
    eliminated = PANEL_COUNT * PANEL_COLUMNS
    result = factor(
        codes, own_rows[0], child_rows, n_front, n_row, n_col, capacity, eliminated
    )
    return result[None]


def solution(mesh):
    placed = (
        P("front", "row", "col"),
        P(("front", "row"), "col"),
        P(("front", "row"), None),
        P(("front", "row")),
    )
    return jax.shard_map(
        body, mesh=mesh, in_specs=placed, out_specs=P("front", "row", "col"), check_vma=False
    )
```

```python
import functools
import jax
import jax.numpy as jnp
from jax import lax
from jax.experimental import pallas as pl
from jax.experimental.pallas import tpu as pltpu
from jax.sharding import PartitionSpec as P

PANEL_COLUMNS = 512
PANEL_COUNT = 2
STAIR_BLK = 128
STAIRS = 8
BLOCK = 128
HALF = 64
TILE = 256
PIECE = 64
LATE = 2
AHEAD = 2
CHUNK = 512
TN = (((0,), (0,)), ((), ()))
NN = (((1,), (0,)), ((), ()))
MESH = pl.DeviceIdType.MESH


def split(x):
    hi = x.astype(jnp.bfloat16)
    return hi, (x - hi.astype(jnp.float32)).astype(jnp.bfloat16)


def dot(a, b, dims):
    return lax.dot_general(a, b, dims, preferred_element_type=jnp.float32)


def dot3(a, b, dims):
    a_hi, a_lo = a
    b_hi, b_lo = b
    return dot(a_lo, b_hi, dims) + dot(a_hi, b_lo, dims) + dot(a_hi, b_hi, dims)


def left_of(x, axis=0):
    hi, lo = split(x)
    return jnp.concatenate([lo, hi, hi], axis)


def right_of(x):
    hi, lo = split(x)
    return jnp.concatenate([hi, lo, hi], 0)


def shift_order(n):
    return sorted(range(1, n), key=lambda s: (-min(s, n - s), s))


def send_order(f, n):
    up, down = list(range(n - 1, f, -1)), list(range(f))
    return down + up if 2 * f < n else up[::-1] + down


def arrival(f, g, n):
    place = send_order(f, n).index(g)
    depth = min(f, n - 1 - f)
    return place + (depth if place >= depth else 0)


def group_tables(n):
    group = {s: q for q, s in enumerate(shift_order(n))}
    sends, takes = [], []
    for f in range(n):
        sends += [group[(g - f) % n] for g in send_order(f, n)]
        sources = [g for g in range(n) if g != f]
        sources.sort(key=lambda g: arrival(g, f, n))
        takes += [group[(f - g) % n] for g in sources]
    return sends, takes


def square_tiles(eliminated, n_col):
    tiles = eliminated // TILE
    packed = [(i, k) for i in range(tiles) for k in range(i, tiles)]
    return [packed[c::n_col] for c in range(n_col)]


def pick(col, values):
    out = values[0]
    for c in range(1, len(values)):
        out = jnp.where(col == c, values[c], out)
    return out


def remote(src, dst, send_sem, recv_sem, device):
    return pltpu.make_async_remote_copy(
        src_ref=src,
        dst_ref=dst,
        send_sem=send_sem,
        recv_sem=recv_sem,
        device_id=device,
        device_id_type=MESH,
    )


def front_kernel(
    n_front, n_row, n_col, cap, codes, own, child, out,
    prod, square, rows, pan, lhs, source, parcel,
    part, other, whole_sq, work, near, far, prev, late_pan,
    zs, zr, ys, yr, here_sem,
    s1, s2, s3, s4, s5, r1, r2, ro_s, ro_r, x_late, own_late, far_late,
):
    f = lax.axis_index("front")
    r = lax.axis_index("row")
    c = lax.axis_index("col")
    n_own, width = own.shape
    eliminated = pan.shape[1]
    order = [0] + shift_order(n_front)
    piece = min(PIECE, cap)
    per = cap // piece
    first = n_own + cap
    count = (n_front - 1) * per

    local = [
        pltpu.make_async_copy(child, source, here_sem.at[0]),
        pltpu.make_async_copy(own, rows.at[pl.ds(0, n_own)], here_sem.at[1]),
    ]
    for copy in local:
        copy.start()
    barrier = pltpu.get_barrier_semaphore()
    for s in range(1, n_front):
        pl.semaphore_signal(
            barrier, inc=1, device_id={"front": (f + s) % n_front}, device_id_type=MESH
        )
    for s in range(1, n_row):
        pl.semaphore_signal(
            barrier, inc=1, device_id={"row": (r + s) % n_row}, device_id_type=MESH
        )
    for s in range(1, n_col):
        pl.semaphore_signal(
            barrier, inc=1, device_id={"col": (c + s) % n_col}, device_id_type=MESH
        )
    pl.semaphore_wait(barrier, n_front + n_row + n_col - 3)

    def z_copy(j, target):
        return remote(
            parcel.at[pl.ds(pl.multiple_of(j * piece, piece), piece)],
            rows.at[pl.ds(pl.multiple_of(first + j * piece, piece), piece)],
            zs.at[j],
            zr.at[j],
            {"front": target},
        )

    sends, takes = group_tables(n_front)

    def y_copy(slot, start, size, other):
        return remote(
            rows.at[pl.ds(start, size), pl.ds(0, eliminated)],
            pan.at[pl.ds(start, size)],
            ys.at[slot, other],
            yr.at[slot],
            {"col": other},
        )

    columns = c * width + lax.broadcasted_iota(jnp.int32, (1, width), 1)

    def pack(into, start, code_start, size):
        def one(i, carry):
            code = codes[code_start + i] - 1
            row = source[pl.ds(jnp.maximum(code, 0) // STAIRS, 1), :]
            edge = jnp.where(code < 0, n_col * width, code % STAIRS * STAIR_BLK)
            into[pl.ds(start + i, 1), :] = jnp.where(columns >= edge, row, 0.0)
            return carry

        lax.fori_loop(0, size, one, 0, unroll=4)

    local[0].wait()

    def post(i, carry):
        j = pick(f * (n_front - 1) + i // per, sends) * per + i % per
        pack(parcel, j * piece, cap + j * piece, piece)
        z_copy(j, (f + pick(j // per, order[1:])) % n_front).start()
        return carry

    lax.fori_loop(0, count, post, 0)
    pack(rows, n_own, 0, cap)

    prod[...] = jnp.zeros_like(prod)
    square[...] = jnp.zeros_like(square)
    work[:, eliminated:] = jnp.zeros((eliminated, work.shape[1] - eliminated), jnp.float32)
    lists = square_tiles(eliminated, n_col)
    slots = len(lists[0])

    def panel(slot, start, size):
        @pl.when(c == 0)
        def _():
            for other in range(1, n_col):
                y_copy(slot, start, size, other).start()
            lhs[pl.ds(0, 3 * size)] = left_of(rows[pl.ds(start, size), pl.ds(0, eliminated)])

        @pl.when(c > 0)
        def _():
            y_copy(slot, start, size, 1).wait_recv()
            lhs[pl.ds(0, 3 * size)] = left_of(pan[pl.ds(start, size)])

    def products(start, size):
        def column(n, carry):
            at = pl.ds(pl.multiple_of(n * TILE, TILE), TILE)
            rhs = right_of(rows[pl.ds(start, size), at])
            for i in range(eliminated // TILE):
                tile = pl.ds(i * TILE, TILE)
                prod[tile, at] += dot(lhs[pl.ds(0, 3 * size), tile], rhs, TN)
            return carry

        lax.fori_loop(0, width // TILE, column, 0)

    def square_dot(a, b, size):
        row = pl.ds(pl.multiple_of(a * TILE, TILE), TILE)
        col = pl.ds(pl.multiple_of(b * TILE, TILE), TILE)
        lo, hi = lhs[pl.ds(0, size), col], lhs[pl.ds(size, size), col]
        return dot(lhs[pl.ds(0, 3 * size), row], jnp.concatenate([hi, lo, hi], 0), TN)

    def consume(slot, start, size):
        panel(slot, start, size)
        products(start, size)
        for j in range(slots):
            a = pick(c, [t[min(j, len(t) - 1)][0] for t in lists])
            b = pick(c, [t[min(j, len(t) - 1)][1] for t in lists])
            square[j] += square_dot(a, b, size)

    local[1].wait()
    consume(0, 0, n_own)
    consume(1, n_own, cap)

    def place(i):
        group = pick(f * (n_front - 1) + i // per, takes)
        return group * per + i % per

    def arrived(i, carry):
        j = place(i)
        z_copy(j, f).wait_recv()
        consume(2 + j, pl.multiple_of(first + j * piece, piece), piece)
        return carry

    lax.fori_loop(0, count - LATE, arrived, 0)
    share = width // n_row
    low = r % 2
    high = r // 2
    mate = r + 1 - 2 * low
    across = r + 2 - 4 * high
    y = n_col - 1 - c
    steps = eliminated // BLOCK
    owner_rows = eliminated // n_row
    half = TILE // 2

    kept = pl.ds(pl.multiple_of(low * half, half), half)
    given = pl.ds(pl.multiple_of((1 - low) * half, half), half)

    def core_copy(j):
        return remote(square.at[j, given], part.at[j], s1.at[0, j], s1.at[1, j], {"row": mate})

    def x_copy(j):
        return remote(part.at[slots + j], other.at[j], s2.at[0, j], s2.at[1, j], {"row": across})

    def flip_copy(j, col):
        tile = whole_sq.at[n_col * j + col, kept]
        return remote(tile, tile, s3.at[0, j], s3.at[1, j], {"col": y})

    def flip_recv(j):
        tile = whole_sq.at[n_col * j + y, kept]
        return remote(tile, tile, s3.at[0, j], s3.at[1, j], {"col": y})

    def mate_copy(j, col, sems):
        tile = whole_sq.at[n_col * j + col, kept]
        return remote(tile, tile, sems.at[0, j], sems.at[1, j], {"row": mate})

    def mate_recv(j, col, sems):
        tile = whole_sq.at[n_col * j + col, given]
        return remote(tile, tile, sems.at[0, j], sems.at[1, j], {"row": mate})

    def near_copy(q, k):
        at = pl.ds(pl.multiple_of(k * BLOCK, BLOCK), BLOCK)
        cols = pl.ds(pl.multiple_of((2 * q + 1 - low) * share, share), share)
        return remote(prod.at[at, cols], near.at[q, at], r1.at[0, q, k], r1.at[1, q, k], {"row": mate})

    theirs = pl.ds(pl.multiple_of((2 * (1 - high) + low) * share, share), share)
    ours = pl.ds(pl.multiple_of((2 * high + low) * share, share), share)

    def far_copy(k):
        at = pl.ds(pl.multiple_of(k * BLOCK, BLOCK), BLOCK)
        return remote(prod.at[at, theirs], far.at[at], r2.at[0, k], r2.at[1, k], {"row": across})

    def late_start(h):
        return pl.multiple_of(first + place(count - LATE + h) * piece, piece)

    def spread(h, source, device, sems):
        return remote(
            source,
            late_pan.at[r, pl.ds(h * piece, piece)],
            sems.at[0, h],
            sems.at[1, h],
            {"row": device},
        )

    def relay(h):
        there = late_pan.at[across, pl.ds(h * piece, piece)]
        return remote(there, there, far_late.at[0, h], far_late.at[1, h], {"row": mate})

    def received(h, source, sems):
        there = late_pan.at[source, pl.ds(h * piece, piece)]
        return remote(there, there, sems.at[0, h], sems.at[1, h], {"row": mate})

    def take(h):
        start = late_start(h)
        j = place(count - LATE + h)
        z_copy(j, f).wait_recv()
        panel(2 + j, start, piece)
        mine = pl.ds(h * piece, piece)

        @pl.when(c == 0)
        def _():
            there = rows.at[pl.ds(start, piece), pl.ds(0, eliminated)]
            spread(h, there, across, x_late).start()
            spread(h, there, mate, own_late).start()
            late_pan[r, mine] = rows[pl.ds(start, piece), pl.ds(0, eliminated)]

        @pl.when(c > 0)
        def _():
            there = pan.at[pl.ds(start, piece)]
            spread(h, there, across, x_late).start()
            spread(h, there, mate, own_late).start()
            late_pan[r, mine] = pan[pl.ds(start, piece)]

        products(start, piece)

    def late_square(h, add):
        received(h, mate, own_late).wait_recv()
        received(h, n_row - 1 - r, far_late).wait_recv()
        size = n_row * piece
        for q in range(n_row):
            hi, lo = split(late_pan[q, pl.ds(h * piece, piece)])
            lhs[pl.ds(q * piece, piece)] = lo
            lhs[pl.ds(size + q * piece, piece)] = hi
            lhs[pl.ds(2 * size + q * piece, piece)] = hi
        for col in range(n_col):
            for j, (a, b) in enumerate(lists[col]):
                tile = slice(a * TILE, (a + 1) * TILE), slice(b * TILE, (b + 1) * TILE)
                value = square_dot(a, b, size)
                if add:
                    value = value + work[tile]
                if h == LATE - 1:
                    value = value + whole_sq[n_col * j + col]
                work[tile] = value

    for j in range(slots):
        core_copy(j).start()
    for j in range(slots):
        core_copy(j).wait_recv()
        part[slots + j] = square[j, kept] + part[j]
        x_copy(j).start()
    for h in range(LATE - 1):
        take(h)
        if h == 0:
            for j in range(slots):
                x_copy(j).wait_recv()
                whole_sq[n_col * j + c, kept] = part[slots + j] + other[j]
                flip_copy(j, c).start()
                mate_copy(j, c, s4).start()
        received(h, across, x_late).wait_recv()
        relay(h).start()
        late_square(h, h > 0)
    take(LATE - 1)

    def hand(k, carry):
        for q in range(n_row // 2):
            near_copy(q, k).start()
        return carry

    for j in range(slots):
        flip_recv(j).wait_recv()
        mate_copy(j, y, s5).start()
    received(LATE - 1, across, x_late).wait_recv()
    relay(LATE - 1).start()
    lax.fori_loop(0, steps, hand, 0)
    for j in range(slots):
        mate_recv(j, c, s4).wait_recv()
        mate_recv(j, y, s5).wait_recv()
    late_square(LATE - 1, LATE > 1)

    def gather(k, carry):
        at = pl.ds(pl.multiple_of(k * BLOCK, BLOCK), BLOCK)
        for q in range(n_row // 2):
            near_copy(q, k).wait_recv()
        prod[at, theirs] += near[1 - high, at]
        far_copy(k).start()
        work[at, pl.ds(eliminated, share)] += prod[at, ours] + near[high, at]
        return carry

    lax.fori_loop(0, AHEAD, gather, 0)

    def result_copy(k):
        at = pl.ds(pl.multiple_of(k * BLOCK, BLOCK), BLOCK)
        owner = k * BLOCK // owner_rows
        inside = pl.ds(pl.multiple_of(k * BLOCK % owner_rows, BLOCK), BLOCK)
        cols = pl.ds(pl.multiple_of(r * share, share), share)
        return remote(
            work.at[at, pl.ds(eliminated, share)],
            out.at[inside, cols],
            ro_s.at[k],
            ro_r.at[r, k % (owner_rows // BLOCK)],
            {"row": owner},
        )

    def result_recv(source, k):
        inside = pl.ds(k * BLOCK, BLOCK)
        cols = pl.ds(pl.multiple_of(source * share, share), share)
        return remote(
            work.at[inside, pl.ds(eliminated, share)],
            out.at[inside, cols],
            ro_s.at[k],
            ro_r.at[source, k],
            {"row": source},
        )

    def deliver(k):
        at = pl.ds(pl.multiple_of(k * BLOCK, BLOCK), BLOCK)
        owner = k * BLOCK // owner_rows

        @pl.when(owner == r)
        def _():
            inside = pl.ds(pl.multiple_of(k * BLOCK % owner_rows, BLOCK), BLOCK)
            out[inside, pl.ds(pl.multiple_of(r * share, share), share)] = work[at, eliminated:]

        @pl.when(owner != r)
        def _():
            result_copy(k).start()

    lanes = lax.broadcasted_iota(jnp.int32, (BLOCK, eliminated), 1)
    total = eliminated + share

    def outer(k, carry):
        at = pl.ds(pl.multiple_of(k * BLOCK, BLOCK), BLOCK)
        lax.fori_loop(
            jnp.minimum(AHEAD * (k + 1), steps), jnp.minimum(AHEAD * (k + 2), steps), gather, 0
        )
        scale = left_of(block_inverse(work[at, at]), 1)
        far_copy(k).wait_recv()
        result = dot(scale, right_of(work[at, eliminated:] + far[at]), NN)
        work[at, eliminated:] = result
        prev[:, eliminated:] = right_of(result)
        top = dot(scale, right_of(work[at, :eliminated]), NN)
        top = jnp.where(lanes >= (k + 1) * BLOCK, top, 0.0)
        prev[:, :eliminated] = right_of(top)
        deliver(k)

        def inner(j, carry):
            rows = pl.ds(pl.multiple_of(j * BLOCK, BLOCK), BLOCK)
            hi, lo = prev[:BLOCK, rows], prev[BLOCK : 2 * BLOCK, rows]
            left = jnp.concatenate([lo, hi, hi], 0)
            for start in range(0, total, CHUNK):
                cols = slice(start, min(total, start + CHUNK))

                @pl.when(j * BLOCK < cols.stop)
                def _():
                    work[rows, cols] -= dot(left, prev[:, cols], TN)

            return carry

        lax.fori_loop(k + 1, steps, inner, 0)
        return carry

    lax.fori_loop(0, steps, outer, 0)

    for s in range(1, n_row):
        for k in range(owner_rows // BLOCK):
            result_recv((r + s) % n_row, k).wait_recv()

    def sent(k, carry):
        far_copy(k).wait_send()

        @pl.when(k * BLOCK // owner_rows != r)
        def _():
            result_copy(k).wait_send()

        return carry

    lax.fori_loop(0, steps, sent, 0)
    for j in range(slots):
        core_copy(j).wait_send()
        x_copy(j).wait_send()
        flip_copy(j, c).wait_send()
        mate_copy(j, c, s4).wait_send()
        mate_copy(j, y, s5).wait_send()
    for h in range(LATE):
        received(h, across, x_late).wait_send()
        received(h, mate, own_late).wait_send()
        relay(h).wait_send()

    def handed(k, carry):
        for q in range(n_row // 2):
            near_copy(q, k).wait_send()
        return carry

    lax.fori_loop(0, steps, handed, 0)

    @pl.when(c == 0)
    def _():
        for other in range(1, n_col):
            y_copy(0, 0, n_own, other).wait_send()
            y_copy(1, n_own, cap, other).wait_send()

            def sent(j, carry):
                start = pl.multiple_of(first + j * piece, piece)
                y_copy(2 + j, start, piece, other).wait_send()
                return carry

            lax.fori_loop(0, count, sent, 0)

    def left(j, carry):
        z_copy(j, f).wait_send()
        return carry

    lax.fori_loop(0, count, left, 0)


def small_inverse(block):
    lanes = lax.broadcasted_iota(jnp.int32, (HALF, HALF), 1)
    rows = lax.broadcasted_iota(jnp.int32, (HALF, HALF), 0)
    eye = (lanes == rows).astype(jnp.float32)
    both = jnp.concatenate([block, eye], 1)
    count = HALF // 8
    groups = [both[g * 8 : (g + 1) * 8] for g in range(count)]
    sub = lax.broadcasted_iota(jnp.int32, (8, 2 * HALF), 0)

    def column_of(g, j):
        return jnp.broadcast_to(groups[g][:, j : j + 1], (8, 2 * HALF))

    def row_of(x, s):
        return jnp.broadcast_to(x[s : s + 1], x.shape)

    for home in range(count):
        first = home * 8
        below = [[column_of(g, first + s) for s in range(8)] for g in range(home + 1, count)]
        columns = [column_of(home, first + s) for s in range(8)]
        solved = forward = groups[home]
        pivot = row_of(columns[0], 0)
        pivots = pivot
        for s in range(8):
            column = columns[s]
            inverse = 1.0 / pivot
            pivots = jnp.where(sub == s, pivot, pivots)
            forward = jnp.where(
                sub > s, forward - column * (row_of(forward, s) * inverse), forward
            )
            scaled = row_of(solved, s) * inverse
            solved = jnp.where(sub == s, scaled, solved - column * scaled)
            for t in range(s + 1, 8):
                row = row_of(columns[t], s)
                fresh = columns[t] - (column * row) * inverse
                if t == s + 1:
                    pivot = row_of(fresh, t)
                columns[t] = jnp.where(sub == s, row * inverse, fresh)
        groups[home] = forward * lax.rsqrt(pivots)
        spread = [row_of(solved, s) for s in range(8)]
        for g in range(home + 1, count):
            terms = [below[g - home - 1][s] * spread[s] for s in range(8)]
            while len(terms) > 1:
                terms = [terms[i] + terms[i + 1] for i in range(0, len(terms), 2)]
            groups[g] = groups[g] - terms[0]
    return jnp.concatenate(groups, 0)[:, HALF:]


def block_inverse(d):
    first = small_inverse(d[:HALF, :HALF])
    first_parts = split(first)
    r12 = dot3(first_parts, split(d[:HALF, HALF:]), NN)
    r12_parts = split(r12)
    second = small_inverse(d[HALF:, HALF:] - dot3(r12_parts, r12_parts, TN))
    corner = -dot3(split(second), split(dot3(r12_parts, first_parts, TN)), NN)
    return jnp.concatenate(
        [
            jnp.concatenate([first, jnp.zeros((HALF, HALF), jnp.float32)], 1),
            jnp.concatenate([corner, second], 1),
        ],
        0,
    )


def factor(codes, own, child, n_front, n_row, n_col, cap, eliminated):
    n_own, width = own.shape
    total = n_own + n_front * cap
    piece = min(PIECE, cap)
    count = (n_front - 1) * (cap // piece)
    slots = len(square_tiles(eliminated, n_col)[0])
    most = max(n_own, cap, n_row * piece)
    share = width // n_row
    steps = eliminated // BLOCK
    owner_rows = eliminated // n_row
    half = TILE // 2
    dma = pltpu.SemaphoreType.DMA
    f32 = jnp.float32
    return pl.pallas_call(
        functools.partial(front_kernel, n_front, n_row, n_col, cap),
        out_shape=jax.ShapeDtypeStruct((owner_rows, width), f32),
        in_specs=[pl.BlockSpec(memory_space=pltpu.SMEM)] + [pl.BlockSpec(memory_space=pl.ANY)] * 2,
        out_specs=pl.BlockSpec(memory_space=pltpu.VMEM),
        scratch_shapes=[
            pltpu.VMEM((eliminated, width), f32),
            pltpu.VMEM((slots, TILE, TILE), f32),
            pltpu.VMEM((total, width), f32),
            pltpu.VMEM((total, eliminated), f32),
            pltpu.VMEM((3 * most, eliminated), jnp.bfloat16),
            pltpu.VMEM(child.shape, f32),
            pltpu.VMEM((count * piece, width), f32),
            pltpu.VMEM((2 * slots, half, TILE), f32),
            pltpu.VMEM((slots, half, TILE), f32),
            pltpu.VMEM((n_col * slots, TILE, TILE), f32),
            pltpu.VMEM((eliminated, eliminated + share), f32),
            pltpu.VMEM((n_row // 2, eliminated, share), f32),
            pltpu.VMEM((eliminated, share), f32),
            pltpu.VMEM((3 * BLOCK, eliminated + share), jnp.bfloat16),
            pltpu.VMEM((n_row, LATE * piece, eliminated), f32),
            dma((count,)),
            dma((count,)),
            dma((count + 2, n_col)),
            dma((count + 2,)),
            dma((2,)),
            dma((2, slots)),
            dma((2, slots)),
            dma((2, slots)),
            dma((2, slots)),
            dma((2, slots)),
            dma((2, n_row // 2, steps)),
            dma((2, steps)),
            dma((steps,)),
            dma((n_row, owner_rows // BLOCK)),
            dma((2, LATE)),
            dma((2, LATE)),
            dma((2, LATE)),
        ],
        compiler_params=pltpu.CompilerParams(
            collective_id=0, has_side_effects=True, vmem_limit_bytes=67043328
        ),
    )(codes, own, child)


def body(own_rows, child_rows, child_dest, child_stair):
    n_front = lax.axis_size("front")
    n_row = lax.axis_size("row")
    n_col = lax.axis_size("col")
    source_rows = child_rows.shape[0]
    capacity = max(2, 2 * source_rows // n_front)
    targets = child_dest[:, 0]
    index = lax.iota(jnp.int32, source_rows)
    ahead = (targets[None, :] == targets[:, None]) & (index[None, :] < index[:, None])
    slot = jnp.sum(ahead.astype(jnp.int32), axis=1)
    shift = (targets - lax.axis_index("front")) % n_front
    rank = jnp.zeros_like(shift)
    for place, s in enumerate(shift_order(n_front)):
        rank = jnp.where(shift == s, place + 1, rank)
    position = rank * capacity + slot
    code = index * STAIRS + child_stair + 1
    places = lax.iota(jnp.int32, n_front * capacity)
    codes = jnp.sum(jnp.where(position[None, :] == places[:, None], code[None, :], 0), axis=1)
    eliminated = PANEL_COUNT * PANEL_COLUMNS
    result = factor(
        codes, own_rows[0], child_rows, n_front, n_row, n_col, capacity, eliminated
    )
    return result[None]


def solution(mesh):
    placed = (
        P("front", "row", "col"),
        P(("front", "row"), "col"),
        P(("front", "row"), None),
        P(("front", "row")),
    )
    return jax.shard_map(
        body, mesh=mesh, in_specs=placed, out_specs=P("front", "row", "col"), check_vma=False
    )
```
